32 devices in a mesh: parts: 2 (over y), freq: 8 (over z, x), seg: 2 (over core).
Axes of the slice: x: 2, y: 2, z: 4, core: 2. Of those that a mesh axis runs over, the one named last changes fastest.
Arguments:
- samples: float32 [8, 2, 1024, 1024], P(('parts', 'seg'), None, 'freq'), parts along dimension 0, may hold values from -6 to 6
- kernels: bfloat16 [2, 8, 128], replicated, may hold values from -0.375 to 0.375
- offsets: int32 [8, 8], P(('parts', 'seg')), parts along dimension 0, may hold values from -4096 to 4096, as said below
- weight_index: int32 [8], P(('parts', 'seg')), parts along dimension 0, may hold values from 0 to 15
- level_weights: float32 [16], replicated, may hold values from 0.1 to 1
Outputs:
- planes: float32 [16, 1048576], P(('parts', 'seg'), 'freq'), parts along dimension 0
The draws below stay inside these ranges and needn't reach their ends.
There are 2 independent parts, one for each index of `parts`. The reference program is written for one: setup_inputs(seed, part) draws one part's arguments, and reference() takes and returns one part's arrays. A program takes and returns all parts, laid end to end along the dimension named above; an argument that names none is the same for every part. Nothing has to cross between parts.
Inputs may be any that keep to these rules, and one draw needn't show every extreme that they name: `offsets`: each offset lies within 4096 blocks of zero; both ends are taken in every draw. Among the 16 offsets of one index of seg, at most 4 have the same quotient by 1024 (rounded down), and in every draw some quotient has exactly 4.
All inputs are finite; a program needn't handle non-finite values.
Results may differ from the reference program's by a relative error of at most 0.01.
Values may be sent and summed in bfloat16 or wider, within the bound.
A program may use at most 128 MiB of HBM per device.

```python
import math
import jax
import jax.numpy as jnp
from jax import lax

N1 = 1024
N2 = 1024
BLOCK = 128
KERNELS = 8
REACH = 4
LEVELS = 16
SEG_DEV = 2
SEGMENTS = 4
BLOCKS_DEV = 1024
ROUTE_CAP = 4


def offsets_group(group_key):
    planes_one = SEG_DEV * KERNELS
    spread = 2 * REACH + 1
    slots = spread * ROUTE_CAP
    centre = jax.random.randint(jax.random.fold_in(group_key, 1), (), -REACH + 1, REACH)
    slot_dist = jnp.repeat(jnp.arange(spread, dtype=jnp.int32) - REACH, ROUTE_CAP)
    slot_rank = jnp.tile(jnp.arange(ROUTE_CAP, dtype=jnp.int32), spread)
    noise = jax.random.permutation(jax.random.fold_in(group_key, 2), slots).astype(jnp.int32)
    extreme = ((slot_dist == REACH) | (slot_dist == -REACH)) & (slot_rank == 0)
    priority = jnp.where(slot_dist == centre, 0, jnp.where(extreme, 1, 2)).astype(jnp.int32)
    order = jnp.argsort(priority * slots + noise, stable=True)
    chosen = slot_dist[order[:planes_one]]
    placing = jax.random.permutation(jax.random.fold_in(group_key, 3), planes_one)
    quotient = jnp.zeros((planes_one,), jnp.int32).at[placing].set(chosen)
    remainder = jax.random.randint(jax.random.fold_in(group_key, 4), (planes_one,), 0, BLOCKS_DEV)
    remainder = jnp.where(jnp.abs(quotient) == REACH, 0, remainder)
    return (quotient * BLOCKS_DEV + remainder).astype(jnp.int32)


def draw_offsets(key, part):
    groups = SEGMENTS // SEG_DEV
    keys = jax.vmap(lambda number: jax.random.fold_in(key, number))(jnp.arange(groups, dtype=jnp.int32) + 11)
    values = jax.vmap(offsets_group)(keys)
    return values.reshape(SEGMENTS, KERNELS).astype(jnp.int32)


def plant(drawn, stream_key, least, top_value):
    index_at = [jax.random.randint(jax.random.fold_in(stream_key, axis), (), 0, length) for axis, length in enumerate(drawn.shape)]
    main_axis = drawn.shape.index(max(drawn.shape))
    neighbour = index_at[:main_axis] + [(index_at[main_axis] + 1) % drawn.shape[main_axis]] + index_at[main_axis + 1:]
    return drawn.at[tuple(index_at)].set(least).at[tuple(neighbour)].set(top_value)


def block_scale(own_key, extent, pieces, low, largest):
    def one(axis_at, shards_of):
        draws = jax.random.uniform(jax.random.fold_in(jax.random.fold_in(own_key, 6), axis_at), (shards_of,), jnp.float32, low / len(pieces), largest / len(pieces))
        return jnp.repeat(jnp.exp(draws), extent[axis_at] // shards_of).reshape((-1,) + (1,) * (len(extent) - axis_at - 1))

    factor_of = one(*pieces[0])
    for cut in pieces[1:]:
        factor_of = factor_of * one(*cut)
    return factor_of


def bell_draw(own_key, extent, width, bound, shards=(), kind=jnp.bfloat16):
    drawn = jax.random.normal(own_key, extent, jnp.float32) * width
    if len(shards) > 0:
        drawn = block_scale(own_key, extent, shards, -0.22, 0.18) * drawn
    return jnp.clip(drawn, min=-bound, max=bound).astype(kind)


def setup_inputs(seed: int = 0, part: int = 0) -> dict:
    streams_of = jax.random.split(jax.random.key(seed), 6)
    own_keys = jax.random.split(jax.random.fold_in(streams_of[5], part), 6)
    samples = bell_draw(own_keys[0], (SEGMENTS, 2, N1, N2), 1.0, 6.0, ((0, 2), (2, 8)), jnp.float32)
    kernels = bell_draw(streams_of[1], (2, KERNELS, BLOCK), (2 * BLOCK) ** -0.5, 0.375)
    offsets = draw_offsets(jax.random.fold_in(jax.random.fold_in(streams_of[5], part), 71), part)
    weight_index = plant(jax.random.randint(own_keys[3], (SEGMENTS,), 0, LEVELS), jax.random.fold_in(own_keys[3], 1), 0, LEVELS - 1).astype(jnp.int32)
    level_weights = jnp.clip(jnp.exp(jax.random.uniform(streams_of[4], (LEVELS,), jnp.float32, math.log(0.1), math.log(1.0))), 0.1, 1.0)
    return dict(samples=samples, kernels=kernels, offsets=offsets, weight_index=weight_index, level_weights=level_weights)


def reference(samples, kernels, offsets, weight_index, level_weights):
    length = N1 * N2
    half = BLOCK // 2
    places = (half - jnp.arange(BLOCK, dtype=jnp.int32)) % length
    kernel_real = kernels[0].astype(jnp.float32)
    kernel_imag = kernels[1].astype(jnp.float32)
    kernel_full = kernel_real + 1j * kernel_imag
    padded = jnp.zeros((KERNELS, length), kernel_full.dtype).at[:, places].set(kernel_full)
    kernel_freq = jnp.fft.fft(padded, axis=-1)
    weights = level_weights[weight_index]

    def roll_blocks(blocks, shift):
        return jnp.roll(blocks, -shift, axis=0)

    def one_segment(total, inputs):
        segment, shifts, weight = inputs
        series = jnp.transpose(segment[0]).reshape(-1) + 1j * jnp.transpose(segment[1]).reshape(-1)
        spectrum = jnp.fft.fft(series) / math.sqrt(length)
        real_part = lax.optimization_barrier(jnp.real(spectrum).astype(jnp.bfloat16)).astype(jnp.float32)
        imag_part = lax.optimization_barrier(jnp.imag(spectrum).astype(jnp.bfloat16)).astype(jnp.float32)
        rounded = real_part + 1j * imag_part
        filtered = jnp.fft.ifft(jnp.fft.fft(rounded)[None, :] * kernel_freq, axis=-1)
        power = jnp.real(filtered) ** 2 + jnp.imag(filtered) ** 2
        power = lax.optimization_barrier(power.astype(jnp.bfloat16)).astype(jnp.float32)
        blocks = power.reshape(KERNELS, length // BLOCK, BLOCK)
        moved = jax.vmap(roll_blocks)(blocks, shifts)
        return (total + weight * moved, None)
    start = jnp.zeros((KERNELS, length // BLOCK, BLOCK), jnp.float32)
    total, unused = lax.scan(one_segment, start, (samples, offsets, weights))
    return (total / SEGMENTS).reshape(KERNELS, length)
```

```python
import math

import functools

import jax
import jax.numpy as jnp
import numpy as np
from jax import lax
from jax.experimental import pallas as pl
from jax.experimental.pallas import tpu as pltpu
from jax.sharding import PartitionSpec as P

BLOCK = 128
KERNELS = 8
REACH = 4
ROUTE_CAP = 4


def extended(cells, sides, width):
    for axis, dim in sides:
        count = lax.axis_size(axis)
        head = lax.slice_in_dim(cells, 0, width, axis=dim)
        tail = lax.slice_in_dim(cells, cells.shape[dim] - width, cells.shape[dim], axis=dim)
        cells = jnp.concatenate(
            [
                lax.ppermute(tail, axis, [(i, (i + 1) % count) for i in range(count)]),
                cells,
                lax.ppermute(head, axis, [((i + 1) % count, i) for i in range(count)]),
            ],
            axis=dim,
        )
    return cells


def passed_along(block, axis, distance):
    devices = range(lax.axis_size(axis))
    route = [((i - distance) % len(devices), i) for i in devices]
    return lax.ppermute(block, axis, route)


def dft_table(size):
    rows = lax.broadcasted_iota(jnp.int32, (size, size), 0)
    cols = lax.broadcasted_iota(jnp.int32, (size, size), 1)
    angle = (rows * cols % size).astype(jnp.float32) * (2.0 * math.pi / size)
    return (jnp.cos(angle), jnp.sin(angle))


def toeplitz(kernels):
    width = kernels.shape[-1]
    tail = jnp.zeros(kernels.shape[:-1] + (width + 1,), kernels.dtype)
    padded = jnp.concatenate([kernels, tail], -1)
    tiled = jnp.tile(padded, (1, 1, width))[..., : 2 * width * width]
    return tiled.reshape(kernels.shape[:-1] + (width, 2 * width))


def take_blocks(joined, start):
    return lax.dynamic_slice_in_dim(joined, start, joined.shape[0] // 2, 0)


def slide(joined, starts):
    return jax.vmap(jax.vmap(take_blocks))(joined, starts)


def general(samples, kernels, offsets, weight_index, level_weights):
    segs, comps, rows_one, cols_two = samples.shape
    ranks = lax.axis_size("freq")
    here = lax.axis_index("freq")
    size_one = rows_one * ranks
    length = size_one * cols_two
    highest = lax.Precision.HIGHEST
    cos_two, sin_two = dft_table(cols_two)
    stacked = samples.reshape(segs * comps * rows_one, cols_two)
    with_cos = jnp.dot(stacked, cos_two, precision=highest).reshape(samples.shape)
    with_sin = jnp.dot(stacked, sin_two, precision=highest).reshape(samples.shape)
    first_real = with_cos[:, 0] + with_sin[:, 1]
    first_imag = with_cos[:, 1] - with_sin[:, 0]
    row_global = here * rows_one + lax.broadcasted_iota(jnp.int32, (rows_one, cols_two), 0)
    col_global = lax.broadcasted_iota(jnp.int32, (rows_one, cols_two), 1)
    twist = (row_global * col_global % length).astype(jnp.float32) * (2.0 * math.pi / length)
    twist_cos = jnp.cos(twist)
    twist_sin = jnp.sin(twist)
    turned = jnp.stack(
        [
            first_real * twist_cos + first_imag * twist_sin,
            first_imag * twist_cos - first_real * twist_sin,
        ],
        1,
    )
    columns = lax.all_to_all(
        turned.astype(jnp.bfloat16), "freq", split_axis=3, concat_axis=3, tiled=True
    ).astype(turned.dtype)
    width_two = cols_two // ranks
    ordered = columns.reshape(segs, comps, rows_one, ranks, width_two)
    cos_one, sin_one = dft_table(size_one)
    cos_one = cos_one.reshape(ranks, rows_one, size_one)
    sin_one = sin_one.reshape(ranks, rows_one, size_one)
    second_cos = jnp.einsum("scirl,rik->sclk", ordered, cos_one, precision=highest)
    second_sin = jnp.einsum("scirl,rik->sclk", ordered, sin_one, precision=highest)
    second = jnp.stack(
        [second_cos[:, 0] + second_sin[:, 1], second_cos[:, 1] - second_sin[:, 0]], 1
    )
    arrived = lax.all_to_all(
        second.astype(jnp.bfloat16), "freq", split_axis=3, concat_axis=3, tiled=True
    ).astype(second.dtype)
    width_one = size_one // ranks
    spectrum = arrived.reshape(segs, comps, width_two, ranks, width_one)
    spectrum = jnp.transpose(spectrum, (0, 1, 4, 3, 2)).reshape(segs, comps, width_one * cols_two)
    spectrum = (spectrum * (1.0 / math.sqrt(length))).astype(jnp.bfloat16)
    half = BLOCK // 2
    edged = extended(spectrum, (("freq", 2),), half)
    bins_here = spectrum.shape[2]
    count = bins_here // BLOCK
    lower = edged[..., :bins_here].reshape(segs, comps, count, BLOCK)
    upper = edged[..., BLOCK:].reshape(segs, comps, count, BLOCK)
    window = jnp.concatenate([lower, upper], -1)
    bands = toeplitz(kernels)
    real_band = bands[0]
    imag_band = bands[1]
    table = jnp.stack(
        [jnp.stack([real_band, imag_band], 0), jnp.stack([-imag_band, real_band], 0)], 0
    )
    filtered = jnp.einsum("scbm,cokim->skboi", window, table, preferred_element_type=jnp.float32)
    power = (filtered[:, :, :, 0] ** 2 + filtered[:, :, :, 1] ** 2).astype(jnp.bfloat16)
    quotient = jnp.floor_divide(offsets, count)
    remainder = offsets - quotient * count
    following = passed_along(power, "freq", -1)
    inner = slide(jnp.concatenate([power, following], 2), remainder)
    plane_count = segs * KERNELS
    flat = inner.reshape(plane_count, count * BLOCK)
    plane_quot = quotient.reshape(plane_count)
    distances = lax.broadcasted_iota(jnp.int32, (2 * REACH + 1, plane_count), 0) - REACH
    member = (plane_quot[None, :] == distances).astype(jnp.int32)
    earlier = lax.broadcasted_iota(jnp.int32, (plane_count, plane_count), 0)
    later = lax.broadcasted_iota(jnp.int32, (plane_count, plane_count), 1)
    place = jnp.sum(jnp.where(earlier <= later, member[:, :, None], 0), 1) - 1
    slot_ids = lax.broadcasted_iota(jnp.int32, (2 * REACH + 1, ROUTE_CAP, plane_count), 1)
    select = ((member[:, None, :] == 1) & (place[:, None, :] == slot_ids)).astype(jnp.bfloat16)
    packed = jnp.einsum("dcp,pl->dcl", select, flat, preferred_element_type=jnp.float32).astype(
        jnp.bfloat16
    )
    received = []
    for step_index in range(2 * REACH + 1):
        received.append(passed_along(packed[step_index], "freq", -(step_index - REACH)))
    gathered = jnp.stack(received, 0)
    placed = jnp.einsum("dcp,dcl->pl", select, gathered, preferred_element_type=jnp.float32)
    shifted = placed.astype(jnp.bfloat16).reshape(segs, KERNELS, count, BLOCK)
    levels = lax.broadcasted_iota(jnp.int32, (segs, level_weights.shape[0]), 1)
    weights = jnp.sum(jnp.where(weight_index[:, None] == levels, level_weights[None, :], 0.0), 1)
    scale = 1.0 / (segs * lax.axis_size("seg"))
    partial_sum = jnp.sum((weights * scale)[:, None, None, None] * shifted.astype(jnp.float32), 0)
    owned = lax.psum_scatter(
        partial_sum.astype(jnp.bfloat16), "seg", scatter_dimension=0, tiled=True
    ).astype(jnp.float32)
    return owned.reshape(owned.shape[0], count * BLOCK)


VMEM = pl.BlockSpec(memory_space=pltpu.VMEM)
SMEM = pl.BlockSpec(memory_space=pltpu.SMEM)
PAD = 16
BF16 = jnp.bfloat16
F32 = jnp.float32


def unit(turns, scale=1.0):
    angle = 2.0 * np.pi * turns
    return (np.cos(angle) * scale).astype(np.float32), (np.sin(angle) * scale).astype(np.float32)


def wave_bases(size, first):
    step = math.isqrt(size)
    while size % step:
        step -= 1
    cols = np.arange(size) + first
    low = np.arange(step)[:, None] * cols[None, :] % size / size
    high = np.arange(size // step)[:, None] * step * cols[None, :] % size / size
    return unit(low) + unit(high)


def fill_waves(low_cos, low_sin, high_cos, high_sin, wave_ref):
    step = low_cos.shape[0]
    each = BLOCK // step

    @pl.loop(0, high_cos.shape[0])
    def _(i):
        hc = high_cos[pl.ds(i, 1), :]
        hs = high_sin[pl.ds(i, 1), :]
        lc = low_cos[...]
        ls = low_sin[...]
        at = i // each * (2 * BLOCK) + i % each * step
        wave_ref[pl.ds(pl.multiple_of(at, step), step), :] = (hc * lc - hs * ls).astype(BF16)
        at = at + BLOCK
        wave_ref[pl.ds(pl.multiple_of(at, step), step), :] = (hs * lc + hc * ls).astype(BF16)


def fill_bands(taps_ref, band_ref):
    wide = 2 * BLOCK
    for t in range(taps_ref.shape[1]):
        both = []
        for c in range(2):
            row = taps_ref[c, t : t + 1, :].astype(F32)
            row = jnp.concatenate([row, jnp.zeros_like(row)], 1)
            row = jnp.broadcast_to(row, (BLOCK, wide))
            both.append(pltpu.roll(row, 0, 1, stride=1, stride_axis=0).T)
        re, im = both
        band_ref[t, :wide, :BLOCK] = re.astype(BF16)
        band_ref[t, :wide, BLOCK:] = im.astype(BF16)
        band_ref[t, wide:, :BLOCK] = (-im).astype(BF16)
        band_ref[t, wide:, BLOCK:] = re.astype(BF16)


def fill_columns(low_cos, low_sin, high_cos, high_sin, table_ref, j):
    step = low_cos.shape[0]
    lanes = pl.ds(pl.multiple_of(j * BLOCK, BLOCK), BLOCK)
    lc = low_cos[:, lanes]
    ls = low_sin[:, lanes]
    for i in range(high_cos.shape[0]):
        hc = high_cos[i : i + 1, lanes]
        hs = high_sin[i : i + 1, lanes]
        rows = slice(i * step, (i + 1) * step)
        table_ref[rows, :BLOCK] = (hc * lc - hs * ls).astype(BF16)
        table_ref[rows, BLOCK:] = (hs * lc + hc * ls).astype(BF16)


def remote(src, dst, sems, at, axis, device):
    return pltpu.make_async_remote_copy(
        src_ref=src,
        dst_ref=dst,
        send_sem=sems[0].at[at],
        recv_sem=sems[1].at[at],
        device_id={axis: device},
        device_id_type=pl.DeviceIdType.MESH,
    )


def first_step(segs, rows, table_ref, xb_ref, near_cos, near_sin, far_ref, j):
    lanes = pl.ds(pl.multiple_of(j * BLOCK, BLOCK), BLOCK)
    got = jnp.dot(xb_ref[...], table_ref[...], preferred_element_type=F32)
    a = far_ref[0:1, lanes]
    b = far_ref[8:9, lanes]
    wc = a * near_cos[:, lanes] - b * near_sin[:, lanes]
    ws = b * near_cos[:, lanes] + a * near_sin[:, lanes]
    out = []
    for s in range(segs):
        top = got[2 * s * rows : (2 * s + 1) * rows]
        low = got[(2 * s + 1) * rows : (2 * s + 2) * rows]
        re = top[:, :BLOCK] + low[:, BLOCK:]
        im = low[:, :BLOCK] - top[:, BLOCK:]
        out += [re * wc + im * ws, im * wc - re * ws]
    return jnp.concatenate(out, 1).astype(BF16)


def second_step(segs, wave_ref, turned_ref, w_ref, j):
    wide = 2 * BLOCK
    total = wave_ref.shape[0] // 2
    tall = w_ref.shape[3] - total

    @pl.loop(0, total // BLOCK)
    def _(i):
        y = jnp.dot(
            wave_ref[pl.ds(pl.multiple_of(i * wide, wide), wide), :], turned_ref[j], preferred_element_type=F32
        )
        here = pl.ds(pl.multiple_of(i * BLOCK, BLOCK), BLOCK)
        for s in range(segs):
            re = slice(s * wide, s * wide + BLOCK)
            im = slice(s * wide + BLOCK, (s + 1) * wide)
            w_ref[s, 0, j, here, :] = (y[:BLOCK, re] + y[BLOCK:, im]).astype(BF16)
            w_ref[s, 1, j, here, :] = (y[:BLOCK, im] - y[BLOCK:, re]).astype(BF16)

    for s in range(segs):
        for c in range(2):
            w_ref[s, c, j, total:, :] = w_ref[s, c, j, :tall, :]


def wrap_column(w_ref, total):
    segs, comps, columns, high, _ = w_ref.shape
    for s in range(segs):
        for c in range(comps):
            x = w_ref[s, c, 0, :total, :].astype(F32)
            w_ref[s, c, columns - 1, :total, :] = jnp.concatenate([x[1:], x[:1]], 0).astype(BF16)
            w_ref[s, c, columns - 1, total:, :] = w_ref[s, c, columns - 1, : high - total, :]


def source_of(off_ref, s, t, total, ranks):
    blocks = total * ranks
    base = lax.rem(lax.axis_index("freq") * total + off_ref[s, t] + blocks, blocks)
    return base // ranks, lax.rem(base, ranks)


def filter_some(w_ref, band_ref, p_ref, power_ref, off_ref, weights, first, columns, rows, ranks):
    segs = len(weights)
    total = rows * ranks
    tall = rows + PAD
    count = band_ref.shape[0]

    @pl.loop(0, count)
    def _(i):
        t = lax.rem(first + i, count)
        parts = []
        shifts = []
        for s in range(segs):
            gk, gj = source_of(off_ref, s, t, total, ranks)
            for j in columns:
                row = lax.rem(gk + (gj - j + ranks - 1) // ranks, total)
                low = row // PAD * PAD
                shifts.append(row - low)
                take = pl.ds(low, tall)
                pieces = [w_ref[s, c, j + e, take, :] for c in range(2) for e in range(2)]
                parts.append(jnp.concatenate(pieces, 1))
        got = jnp.dot(jnp.concatenate(parts, 0), band_ref[t], preferred_element_type=F32)
        re = got[:, :BLOCK]
        im = got[:, BLOCK:]
        p_ref[...] = re * re + im * im
        for s in range(segs):
            for n, j in enumerate(columns):
                at = s * len(columns) + n
                x = p_ref[pl.ds(at * tall + shifts[at], rows), :]
                power_ref[i, s, j] = (weights[s] * x).astype(BF16)


def gather_kernel(
    marks,
    x_hbm, table_hbm, taps_hbm, off_ref, wi_ref, lw_ref,
    power_ref, got_ref,
    x_ref, base_ref, taps_ref, table_ref, wave_ref, xb_ref, far_ref, turned_ref, w_ref, band_ref, p_ref, send_ref,
    in_sem,
    ring_send, ring_recv, core_send, core_recv,
):
    segs, comps, rows, cols = x_ref.shape
    ranks = lax.axis_size("freq")
    total = rows * ranks
    hops = ranks // 2
    lead = 3
    me = lax.axis_index("freq")
    core = lax.axis_index("seg")
    half = got_ref.shape[0]
    weights = [lw_ref[wi_ref[s]] * (1.0 / (2 * segs)) for s in range(segs)]

    fetch_x = pltpu.make_async_copy(x_hbm, x_ref, in_sem.at[0])
    fetch_x.start()
    fetch_base = pltpu.make_async_copy(table_hbm, base_ref, in_sem.at[1])
    fetch_base.start()
    fetch_taps = pltpu.make_async_copy(taps_hbm, taps_ref, in_sem.at[2])
    fetch_taps.start()
    bases = [base_ref.at[marks[i] : marks[i + 1], :] for i in range(len(marks) - 1)]
    b_bases = bases[:4]
    e_bases = bases[4:8]
    near_cos, near_sin, far_cos, far_sin = bases[8:]

    odd = me % 2
    place = (1 - odd) * (me // 2) + odd * (ranks - 1 - me // 2)

    def at_place(p):
        p = (p + ranks) % ranks
        far = p // (ranks // 2)
        return (1 - far) * (2 * p) + far * (2 * (ranks - 1 - p) + 1)

    barrier = pltpu.get_barrier_semaphore()
    for peer in (at_place(place + 1), at_place(place - 1)):
        pl.semaphore_signal(barrier, inc=1, device_id={"freq": peer}, device_id_type=pl.DeviceIdType.MESH)
    pl.semaphore_signal(barrier, inc=1, device_id={"seg": 1 - core}, device_id_type=pl.DeviceIdType.MESH)

    def moved(j, k, way, origin):
        owner = at_place(place - origin) if way == 0 else at_place(place + origin)
        target = at_place(place + 1) if way == 0 else at_place(place - 1)
        size = rows if k < hops - 1 else rows // 2
        start = owner * rows + (0 if k < hops - 1 else way * size)
        block = turned_ref.at[j, pl.ds(pl.multiple_of(start, size), size), :]
        return remote(block, block, (ring_send, ring_recv), (way, j, k), "freq", target)

    def send(j, k):
        for way in range(2):
            moved(j, k, way, k).start()

    def landed(j, k):
        for way in range(2):
            moved(j, k, way, k + 1).wait_recv()

    fetch_x.wait()
    for s in range(segs):
        for c in range(comps):
            at = (s * comps + c) * rows
            xb_ref[at : at + rows, :] = x_ref[s, c].astype(BF16)
    fetch_base.wait()
    far_ref[0:1, :] = far_cos[pl.ds(me, 1), :]
    far_ref[8:9, :] = far_sin[pl.ds(me, 1), :]
    own_rows = pl.ds(pl.multiple_of(me * rows, rows), rows)

    @pl.loop(0, ranks)
    def _(j):
        fill_columns(*b_bases, table_ref, j)
        turned_ref[j, own_rows, :] = first_step(segs, rows, table_ref, xb_ref, near_cos, near_sin, far_ref, j)

        @pl.when(j == 0)
        def _():
            pl.semaphore_wait(barrier, 3)

        @pl.when(j < lead)
        def _():
            send(j, 0)

    fill_waves(*e_bases, wave_ref)
    fetch_taps.wait()
    fill_bands(taps_ref, band_ref)

    sift = functools.partial(filter_some, w_ref, band_ref, p_ref, power_ref, off_ref, weights, core * half)

    @pl.loop(0, ranks + 1)
    def _(q):
        @pl.when(q < ranks)
        def _():
            landed(q, 0)
            send(q, 1)

        @pl.when(q < ranks - lead)
        def _():
            send(q + lead, 0)

        @pl.when(q >= 1)
        def _():
            landed(q - 1, 2)
            send(q - 1, 3)

        for pair in range(ranks // 2 - 1):

            @pl.when(q == 2 * pair + 4)
            def _():
                sift((2 * pair, 2 * pair + 1), rows, ranks)

        @pl.when(q < ranks)
        def _():
            landed(q, 1)
            send(q, 2)

        @pl.when(q >= 1)
        def _():
            landed(q - 1, 3)
            second_step(segs, wave_ref, turned_ref, w_ref, q - 1)

        @pl.when(q == 1)
        def _():
            wrap_column(w_ref, total)

    sift((ranks - 2, ranks - 1), rows, ranks)

    def swap(i):
        return remote(send_ref.at[i], got_ref.at[i], (core_send, core_recv), (i,), "seg", 1 - core)

    for i in range(half):
        t = (1 - core) * half + i
        turns = [source_of(off_ref, s, t, total, ranks)[1] for s in range(segs)]
        for jj in range(ranks):
            x = sum(power_ref[half + i, s, lax.rem(turns[s] + jj, ranks)].astype(F32) for s in range(segs))
            send_ref[i, jj] = x.astype(BF16)
        swap(i).start()
    for i in range(half):
        swap(i).wait()

    @pl.loop(0, ranks)
    def _(j):
        for k in range(hops):
            for way in range(2):
                moved(j, k, way, k).wait_send()


def combine_kernel(off_ref, power_ref, got_ref, out_ref):
    half, ranks, rows, _ = got_ref.shape
    segs = power_ref.shape[1]
    core = lax.axis_index("seg")

    @pl.loop(0, half)
    def _(i):
        turns = [source_of(off_ref, s, core * half + i, rows * ranks, ranks)[1] for s in range(segs)]
        for jj in range(ranks):
            x = got_ref[i, jj].astype(F32)
            for s in range(segs):
                x = x + power_ref[i, s, lax.rem(turns[s] + jj, ranks)].astype(F32)
            out_ref[i, :, jj * BLOCK : (jj + 1) * BLOCK] = x


def body(samples, kernels, offsets, weight_index, level_weights):
    segs, comps, rows, cols = samples.shape
    ranks = lax.axis_size("freq")
    size_one = rows * ranks
    if cols != ranks * BLOCK or rows != BLOCK or size_one != cols or segs != 2 or lax.axis_size("seg") != 2:
        return general(samples, kernels, offsets, weight_index, level_weights)
    length = size_one * cols
    bins = np.arange(cols) - BLOCK // 2
    near = unit(np.arange(rows)[:, None] * bins[None, :] % length / length, 1.0 / math.sqrt(length))
    far = unit(np.arange(ranks)[:, None] * rows * bins[None, :] % length / length)
    count = kernels.shape[1]
    half = count // 2
    tall = rows + PAD
    hops = ranks // 2
    copies = pltpu.SemaphoreType.DMA
    tables = (*wave_bases(cols, -(BLOCK // 2)), *wave_bases(size_one, 0), *near, *far)
    marks = np.cumsum([0] + [len(x) for x in tables]).tolist()
    power, got = pl.pallas_call(
        functools.partial(gather_kernel, marks),
        out_shape=(
            jax.ShapeDtypeStruct((count, segs, ranks, rows, BLOCK), BF16),
            jax.ShapeDtypeStruct((half, ranks, rows, BLOCK), BF16),
        ),
        in_specs=[pl.BlockSpec(memory_space=pltpu.HBM)] * 3 + [SMEM] * 3,
        out_specs=(VMEM, VMEM),
        scratch_shapes=[
            pltpu.VMEM(samples.shape, F32),
            pltpu.VMEM((marks[-1], cols), F32),
            pltpu.VMEM(kernels.shape, kernels.dtype),
            pltpu.VMEM((cols, 2 * BLOCK), BF16),
            pltpu.VMEM((2 * size_one, size_one), BF16),
            pltpu.VMEM((segs * comps * rows, cols), BF16),
            pltpu.VMEM((16, cols), F32),
            pltpu.VMEM((ranks, size_one, segs * comps * BLOCK), BF16),
            pltpu.VMEM((segs, comps, ranks + 1, size_one + tall, BLOCK), BF16),
            pltpu.VMEM((count, 4 * BLOCK, 2 * BLOCK), BF16),
            pltpu.VMEM((2 * segs * tall, BLOCK), F32),
            pltpu.VMEM((half, ranks, rows, BLOCK), BF16),
        ]
        + [copies((3,))]
        + [copies((2, ranks, hops))] * 2
        + [copies((half,))] * 2,
        compiler_params=pltpu.CompilerParams(vmem_limit_bytes=48 << 20, collective_id=0, has_side_effects=True),
    )(
        pltpu.with_memory_space_constraint(samples, pltpu.HBM),
        pltpu.with_memory_space_constraint(jnp.asarray(np.concatenate(tables)), pltpu.HBM),
        pltpu.with_memory_space_constraint(kernels, pltpu.HBM),
        offsets,
        weight_index,
        level_weights,
    )
    out = pl.pallas_call(
        combine_kernel,
        out_shape=jax.ShapeDtypeStruct((half, rows, cols), F32),
        in_specs=[SMEM, VMEM, VMEM],
        out_specs=VMEM,
        compiler_params=pltpu.CompilerParams(vmem_limit_bytes=24 << 20),
    )(offsets, power, got)
    return out.reshape(half, rows * cols)


def solution(mesh):
    in_specs = (
        P(("parts", "seg"), None, "freq", None),
        P(),
        P(("parts", "seg"), None),
        P(("parts", "seg")),
        P(),
    )
    out_specs = P(("parts", "seg"), "freq")
    return jax.shard_map(body, mesh=mesh, in_specs=in_specs, out_specs=out_specs, check_vma=False)
```

```python
import math

import functools

import jax
import jax.numpy as jnp
import numpy as np
from jax import lax
from jax.experimental import pallas as pl
from jax.experimental.pallas import tpu as pltpu
from jax.sharding import PartitionSpec as P

BLOCK = 128
KERNELS = 8
REACH = 4
ROUTE_CAP = 4


def extended(cells, sides, width):
    for axis, dim in sides:
        count = lax.axis_size(axis)
        head = lax.slice_in_dim(cells, 0, width, axis=dim)
        tail = lax.slice_in_dim(cells, cells.shape[dim] - width, cells.shape[dim], axis=dim)
        cells = jnp.concatenate(
            [
                lax.ppermute(tail, axis, [(i, (i + 1) % count) for i in range(count)]),
                cells,
                lax.ppermute(head, axis, [((i + 1) % count, i) for i in range(count)]),
            ],
            axis=dim,
        )
    return cells


def passed_along(block, axis, distance):
    devices = range(lax.axis_size(axis))
    route = [((i - distance) % len(devices), i) for i in devices]
    return lax.ppermute(block, axis, route)


def dft_table(size):
    rows = lax.broadcasted_iota(jnp.int32, (size, size), 0)
    cols = lax.broadcasted_iota(jnp.int32, (size, size), 1)
    angle = (rows * cols % size).astype(jnp.float32) * (2.0 * math.pi / size)
    return (jnp.cos(angle), jnp.sin(angle))


def toeplitz(kernels):
    width = kernels.shape[-1]
    tail = jnp.zeros(kernels.shape[:-1] + (width + 1,), kernels.dtype)
    padded = jnp.concatenate([kernels, tail], -1)
    tiled = jnp.tile(padded, (1, 1, width))[..., : 2 * width * width]
    return tiled.reshape(kernels.shape[:-1] + (width, 2 * width))


def take_blocks(joined, start):
    return lax.dynamic_slice_in_dim(joined, start, joined.shape[0] // 2, 0)


def slide(joined, starts):
    return jax.vmap(jax.vmap(take_blocks))(joined, starts)


def general(samples, kernels, offsets, weight_index, level_weights):
    segs, comps, rows_one, cols_two = samples.shape
    ranks = lax.axis_size("freq")
    here = lax.axis_index("freq")
    size_one = rows_one * ranks
    length = size_one * cols_two
    highest = lax.Precision.HIGHEST
    cos_two, sin_two = dft_table(cols_two)
    stacked = samples.reshape(segs * comps * rows_one, cols_two)
    with_cos = jnp.dot(stacked, cos_two, precision=highest).reshape(samples.shape)
    with_sin = jnp.dot(stacked, sin_two, precision=highest).reshape(samples.shape)
    first_real = with_cos[:, 0] + with_sin[:, 1]
    first_imag = with_cos[:, 1] - with_sin[:, 0]
    row_global = here * rows_one + lax.broadcasted_iota(jnp.int32, (rows_one, cols_two), 0)
    col_global = lax.broadcasted_iota(jnp.int32, (rows_one, cols_two), 1)
    twist = (row_global * col_global % length).astype(jnp.float32) * (2.0 * math.pi / length)
    twist_cos = jnp.cos(twist)
    twist_sin = jnp.sin(twist)
    turned = jnp.stack(
        [
            first_real * twist_cos + first_imag * twist_sin,
            first_imag * twist_cos - first_real * twist_sin,
        ],
        1,
    )
    columns = lax.all_to_all(
        turned.astype(jnp.bfloat16), "freq", split_axis=3, concat_axis=3, tiled=True
    ).astype(turned.dtype)
    width_two = cols_two // ranks
    ordered = columns.reshape(segs, comps, rows_one, ranks, width_two)
    cos_one, sin_one = dft_table(size_one)
    cos_one = cos_one.reshape(ranks, rows_one, size_one)
    sin_one = sin_one.reshape(ranks, rows_one, size_one)
    second_cos = jnp.einsum("scirl,rik->sclk", ordered, cos_one, precision=highest)
    second_sin = jnp.einsum("scirl,rik->sclk", ordered, sin_one, precision=highest)
    second = jnp.stack(
        [second_cos[:, 0] + second_sin[:, 1], second_cos[:, 1] - second_sin[:, 0]], 1
    )
    arrived = lax.all_to_all(
        second.astype(jnp.bfloat16), "freq", split_axis=3, concat_axis=3, tiled=True
    ).astype(second.dtype)
    width_one = size_one // ranks
    spectrum = arrived.reshape(segs, comps, width_two, ranks, width_one)
    spectrum = jnp.transpose(spectrum, (0, 1, 4, 3, 2)).reshape(segs, comps, width_one * cols_two)
    spectrum = (spectrum * (1.0 / math.sqrt(length))).astype(jnp.bfloat16)
    half = BLOCK // 2
    edged = extended(spectrum, (("freq", 2),), half)
    bins_here = spectrum.shape[2]
    count = bins_here // BLOCK
    lower = edged[..., :bins_here].reshape(segs, comps, count, BLOCK)
    upper = edged[..., BLOCK:].reshape(segs, comps, count, BLOCK)
    window = jnp.concatenate([lower, upper], -1)
    bands = toeplitz(kernels)
    real_band = bands[0]
    imag_band = bands[1]
    table = jnp.stack(
        [jnp.stack([real_band, imag_band], 0), jnp.stack([-imag_band, real_band], 0)], 0
    )
    filtered = jnp.einsum("scbm,cokim->skboi", window, table, preferred_element_type=jnp.float32)
    power = (filtered[:, :, :, 0] ** 2 + filtered[:, :, :, 1] ** 2).astype(jnp.bfloat16)
    quotient = jnp.floor_divide(offsets, count)
    remainder = offsets - quotient * count
    following = passed_along(power, "freq", -1)
    inner = slide(jnp.concatenate([power, following], 2), remainder)
    plane_count = segs * KERNELS
    flat = inner.reshape(plane_count, count * BLOCK)
    plane_quot = quotient.reshape(plane_count)
    distances = lax.broadcasted_iota(jnp.int32, (2 * REACH + 1, plane_count), 0) - REACH
    member = (plane_quot[None, :] == distances).astype(jnp.int32)
    earlier = lax.broadcasted_iota(jnp.int32, (plane_count, plane_count), 0)
    later = lax.broadcasted_iota(jnp.int32, (plane_count, plane_count), 1)
    place = jnp.sum(jnp.where(earlier <= later, member[:, :, None], 0), 1) - 1
    slot_ids = lax.broadcasted_iota(jnp.int32, (2 * REACH + 1, ROUTE_CAP, plane_count), 1)
    select = ((member[:, None, :] == 1) & (place[:, None, :] == slot_ids)).astype(jnp.bfloat16)
    packed = jnp.einsum("dcp,pl->dcl", select, flat, preferred_element_type=jnp.float32).astype(
        jnp.bfloat16
    )
    received = []
    for step_index in range(2 * REACH + 1):
        received.append(passed_along(packed[step_index], "freq", -(step_index - REACH)))
    gathered = jnp.stack(received, 0)
    placed = jnp.einsum("dcp,dcl->pl", select, gathered, preferred_element_type=jnp.float32)
    shifted = placed.astype(jnp.bfloat16).reshape(segs, KERNELS, count, BLOCK)
    levels = lax.broadcasted_iota(jnp.int32, (segs, level_weights.shape[0]), 1)
    weights = jnp.sum(jnp.where(weight_index[:, None] == levels, level_weights[None, :], 0.0), 1)
    scale = 1.0 / (segs * lax.axis_size("seg"))
    partial_sum = jnp.sum((weights * scale)[:, None, None, None] * shifted.astype(jnp.float32), 0)
    owned = lax.psum_scatter(
        partial_sum.astype(jnp.bfloat16), "seg", scatter_dimension=0, tiled=True
    ).astype(jnp.float32)
    return owned.reshape(owned.shape[0], count * BLOCK)


VMEM = pl.BlockSpec(memory_space=pltpu.VMEM)
SMEM = pl.BlockSpec(memory_space=pltpu.SMEM)
PAD = 16
RADIX = 4
LEAD = 4
BF16 = jnp.bfloat16
F32 = jnp.float32


def unit(turns, scale=1.0):
    angle = 2.0 * np.pi * turns
    return (np.cos(angle) * scale).astype(np.float32), (np.sin(angle) * scale).astype(np.float32)


def first_waves(size):
    turns = np.arange(size)[:, None] * (np.arange(size) - BLOCK // 2)[None, :] % size / size
    both = np.stack([x.reshape(size, size // BLOCK, BLOCK) for x in unit(turns)], 2)
    return np.transpose(both, (1, 0, 2, 3)).reshape(size // BLOCK, size, 2 * BLOCK).astype(BF16)


def second_waves(size):
    quarter = size // RADIX
    places = np.arange(quarter)[None, None, :] * RADIX + np.arange(RADIX)[:, None, None]
    turns = np.arange(quarter)[None, :, None] * places % size / size
    return np.concatenate(unit(turns), 1).astype(BF16)


def fill_bands(taps_ref, band_ref):
    wide = 2 * BLOCK
    for t in range(taps_ref.shape[1]):
        both = []
        for c in range(2):
            row = taps_ref[c, t : t + 1, :].astype(F32)
            row = jnp.concatenate([row, jnp.zeros_like(row)], 1)
            row = jnp.broadcast_to(row, (BLOCK, wide))
            both.append(pltpu.roll(row, 0, 1, stride=1, stride_axis=0).T)
        re, im = both
        band_ref[t, :wide, :BLOCK] = re.astype(BF16)
        band_ref[t, :wide, BLOCK:] = im.astype(BF16)
        band_ref[t, wide:, :BLOCK] = (-im).astype(BF16)
        band_ref[t, wide:, BLOCK:] = re.astype(BF16)


def remote(src, dst, sems, at, axis, device):
    return pltpu.make_async_remote_copy(
        src_ref=src,
        dst_ref=dst,
        send_sem=sems[0].at[at],
        recv_sem=sems[1].at[at],
        device_id={axis: device},
        device_id_type=pl.DeviceIdType.MESH,
    )


def first_step(segs, rows, table_ref, xb_ref, near_cos, near_sin, far_ref, mixed_ref, j):
    lanes = pl.ds(pl.multiple_of(j * BLOCK, BLOCK), BLOCK)
    got = jnp.dot(xb_ref[...], table_ref[j], preferred_element_type=F32)
    a = far_ref[0:1, lanes]
    b = far_ref[8:9, lanes]
    wc = a * near_cos[:, lanes] - b * near_sin[:, lanes]
    ws = b * near_cos[:, lanes] + a * near_sin[:, lanes]
    for s in range(segs):
        top = got[2 * s * rows : (2 * s + 1) * rows]
        low = got[(2 * s + 1) * rows : (2 * s + 2) * rows]
        re = top[:, :BLOCK] + low[:, BLOCK:]
        im = low[:, :BLOCK] - top[:, BLOCK:]
        mixed_ref[2 * s] = re * wc + im * ws
        mixed_ref[2 * s + 1] = im * wc - re * ws


def second_step(segs, wave_ref, turned_ref, w_ref, j):
    wide = 2 * BLOCK
    quarter = wave_ref.shape[1] // 2
    total = quarter * RADIX
    tall = w_ref.shape[3] - total
    for s in range(segs):
        terms = []
        for c in range(RADIX):
            y = jnp.dot(
                wave_ref[c], turned_ref[j, c, :, s * wide : (s + 1) * wide], preferred_element_type=F32
            )
            re = y[:quarter, :BLOCK] + y[quarter:, BLOCK:]
            im = y[:quarter, BLOCK:] - y[quarter:, :BLOCK]
            terms.append((re, im))
        (r0, i0), (r1, i1), (r2, i2), (r3, i3) = terms
        re = (r0 + r2) + (r1 + r3), (r0 - r2) + (i1 - i3), (r0 + r2) - (r1 + r3), (r0 - r2) - (i1 - i3)
        im = (i0 + i2) + (i1 + i3), (i0 - i2) - (r1 - r3), (i0 + i2) - (i1 + i3), (i0 - i2) + (r1 - r3)
        for m in range(RADIX):
            here = slice(m * quarter, (m + 1) * quarter)
            w_ref[s, 0, j, here, :] = re[m].astype(BF16)
            w_ref[s, 1, j, here, :] = im[m].astype(BF16)
        for c in range(2):
            w_ref[s, c, j, total:, :] = w_ref[s, c, j, :tall, :]


def wrap_column(w_ref, total):
    segs, comps, columns, high, _ = w_ref.shape
    for s in range(segs):
        for c in range(comps):
            x = w_ref[s, c, 0, :total, :].astype(F32)
            w_ref[s, c, columns - 1, :total, :] = jnp.concatenate([x[1:], x[:1]], 0).astype(BF16)
            w_ref[s, c, columns - 1, total:, :] = w_ref[s, c, columns - 1, : high - total, :]


def source_of(off_ref, s, t, total, ranks):
    blocks = total * ranks
    base = lax.rem(lax.axis_index("freq") * total + off_ref[s, t] + blocks, blocks)
    return base // ranks, lax.rem(base, ranks)


def filter_some(w_ref, band_ref, p_ref, power_ref, off_ref, weights, first, columns, rows, ranks, low, high):
    segs = len(weights)
    total = rows * ranks
    tall = rows + PAD
    count = band_ref.shape[0]

    @pl.loop(low, high)
    def _(i):
        t = lax.rem(first + i, count)
        parts = []
        shifts = []
        for s in range(segs):
            gk, gj = source_of(off_ref, s, t, total, ranks)
            for j in columns:
                row = lax.rem(gk + (gj - j + ranks - 1) // ranks, total)
                start = row // PAD * PAD
                shifts.append(row - start)
                take = pl.ds(start, tall)
                pieces = [w_ref[s, c, j + e, take, :] for c in range(2) for e in range(2)]
                parts.append(jnp.concatenate(pieces, 1))
        got = jnp.dot(jnp.concatenate(parts, 0), band_ref[t], preferred_element_type=F32)
        re = got[:, :BLOCK]
        im = got[:, BLOCK:]
        p_ref[...] = re * re + im * im
        for s in range(segs):
            for n, j in enumerate(columns):
                at = s * len(columns) + n
                x = p_ref[pl.ds(at * tall + shifts[at], rows), :]
                power_ref[i, s, j] = (weights[s] * x).astype(BF16)


def gather_kernel(
    marks,
    x_hbm, first_hbm, base_hbm, wave_hbm, taps_hbm, off_hbm, wi_hbm, lw_hbm,
    power_ref, got_ref,
    x_ref, table_ref, base_ref, wave_ref, taps_ref, off_ref, wi_ref, lw_ref,
    xb_ref, far_ref, mixed_ref, turned_ref, w_ref, band_ref, p_ref, send_ref,
    in_sem, column_sem,
    ring_send, ring_recv, core_send, core_recv,
):
    segs, comps, rows, cols = x_ref.shape
    ranks = lax.axis_size("freq")
    total = rows * ranks
    hops = ranks // 2
    part = rows // RADIX
    me = lax.axis_index("freq")
    core = lax.axis_index("seg")
    half = got_ref.shape[0]

    def fetch_column(j):
        return pltpu.make_async_copy(first_hbm.at[j], table_ref.at[j], column_sem.at[j])

    fetches = [
        pltpu.make_async_copy(src, dst, in_sem.at[n])
        for n, (src, dst) in enumerate(
            [
                (x_hbm, x_ref), (base_hbm, base_ref), (off_hbm, off_ref), (wi_hbm, wi_ref),
                (lw_hbm, lw_ref), (taps_hbm, taps_ref), (wave_hbm, wave_ref),
            ]
        )
    ]
    fetches[0].start()
    fetch_column(0).start()
    fetches[1].start()
    for j in range(1, ranks):
        fetch_column(j).start()
    for fetch in fetches[2:]:
        fetch.start()

    near_cos, near_sin, far_cos, far_sin = [base_ref.at[marks[i] : marks[i + 1], :] for i in range(len(marks) - 1)]

    odd = me % 2
    place = (1 - odd) * (me // 2) + odd * (ranks - 1 - me // 2)

    def at_place(p):
        p = (p + ranks) % ranks
        far = p // (ranks // 2)
        return (1 - far) * (2 * p) + far * (2 * (ranks - 1 - p) + 1)

    barrier = pltpu.get_barrier_semaphore()
    for peer in (at_place(place + 1), at_place(place - 1)):
        pl.semaphore_signal(barrier, inc=1, device_id={"freq": peer}, device_id_type=pl.DeviceIdType.MESH)
    pl.semaphore_signal(barrier, inc=1, device_id={"seg": 1 - core}, device_id_type=pl.DeviceIdType.MESH)

    def moved(j, k, way, origin):
        owner = at_place(place - origin) if way == 0 else at_place(place + origin)
        target = at_place(place + 1) if way == 0 else at_place(place - 1)
        classes = pl.ds(0, RADIX) if k < hops - 1 else pl.ds(way * (RADIX // 2), RADIX // 2)
        block = turned_ref.at[j, classes, pl.ds(pl.multiple_of(owner * part, part), part), :]
        return remote(block, block, (ring_send, ring_recv), (way, j, k), "freq", target)

    def send(j, k):
        for way in range(2):
            moved(j, k, way, k).start()

    def landed(j, k):
        for way in range(2):
            moved(j, k, way, k + 1).wait_recv()

    own_rows = pl.ds(pl.multiple_of(me * part, part), part)
    fetches[0].wait()
    for s in range(segs):
        for c in range(comps):
            at = (s * comps + c) * rows
            xb_ref[at : at + rows, :] = x_ref[s, c].astype(BF16)
    fetches[1].wait()
    far_ref[0:1, :] = far_cos[pl.ds(me, 1), :]
    far_ref[8:9, :] = far_sin[pl.ds(me, 1), :]

    @pl.loop(0, ranks)
    def _(j):
        fetch_column(j).wait()
        first_step(segs, rows, table_ref, xb_ref, near_cos, near_sin, far_ref, mixed_ref, j)
        for n in range(RADIX):
            for i in range(segs * comps):
                lanes = slice(i * BLOCK, (i + 1) * BLOCK)
                turned_ref[j, n, own_rows, lanes] = mixed_ref[i, pl.ds(n, part, stride=RADIX), :].astype(BF16)

        @pl.when(j == 0)
        def _():
            pl.semaphore_wait(barrier, 3)

        @pl.when(j < LEAD)
        def _():
            send(j, 0)

    for fetch in fetches[2:]:
        fetch.wait()
    weights = [lw_ref[wi_ref[s]] * (1.0 / (2 * segs)) for s in range(segs)]
    sift = functools.partial(filter_some, w_ref, band_ref, p_ref, power_ref, off_ref, weights, core * half)

    @pl.loop(0, ranks + 1)
    def _(q):
        @pl.when(q < ranks)
        def _():
            landed(q, 0)
            send(q, 1)

        @pl.when(q < ranks - LEAD)
        def _():
            send(q + LEAD, 0)

        @pl.when(q == 0)
        def _():
            fill_bands(taps_ref, band_ref)

        @pl.when(q >= 1)
        def _():
            landed(q - 1, 2)
            send(q - 1, 3)

        for pair in range(ranks // 2 - 1):

            @pl.when(q == 2 * pair + 4)
            def _():
                sift((2 * pair, 2 * pair + 1), rows, ranks, 0, 2 * half)

        @pl.when(q < ranks)
        def _():
            landed(q, 1)
            send(q, 2)

        @pl.when(q >= 1)
        def _():
            landed(q - 1, 3)
            second_step(segs, wave_ref, turned_ref, w_ref, q - 1)

        @pl.when(q == 1)
        def _():
            wrap_column(w_ref, total)

    def swap(i):
        return remote(send_ref.at[i], got_ref.at[i], (core_send, core_recv), (i,), "seg", 1 - core)

    @pl.loop(0, half)
    def _(i):
        sift((ranks - 2, ranks - 1), rows, ranks, half + i, half + i + 1)
        t = (1 - core) * half + i
        turns = [source_of(off_ref, s, t, total, ranks)[1] for s in range(segs)]
        for jj in range(ranks):
            x = sum(power_ref[half + i, s, lax.rem(turns[s] + jj, ranks)].astype(F32) for s in range(segs))
            send_ref[i, jj] = x.astype(BF16)
        swap(i).start()

    sift((ranks - 2, ranks - 1), rows, ranks, 0, half)

    @pl.loop(0, half)
    def _(i):
        swap(i).wait()

    @pl.loop(0, ranks)
    def _(j):
        for k in range(hops):
            for way in range(2):
                moved(j, k, way, k).wait_send()


def combine_kernel(off_ref, power_ref, got_ref, out_ref):
    half, ranks, rows, _ = got_ref.shape
    segs = power_ref.shape[1]
    core = lax.axis_index("seg")

    @pl.loop(0, half)
    def _(i):
        turns = [source_of(off_ref, s, core * half + i, rows * ranks, ranks)[1] for s in range(segs)]
        for jj in range(ranks):
            x = got_ref[i, jj].astype(F32)
            for s in range(segs):
                x = x + power_ref[i, s, lax.rem(turns[s] + jj, ranks)].astype(F32)
            out_ref[i, :, jj * BLOCK : (jj + 1) * BLOCK] = x


def body(samples, kernels, offsets, weight_index, level_weights):
    segs, comps, rows, cols = samples.shape
    ranks = lax.axis_size("freq")
    size_one = rows * ranks
    if cols != ranks * BLOCK or rows != BLOCK or size_one != cols or segs != 2 or lax.axis_size("seg") != 2:
        return general(samples, kernels, offsets, weight_index, level_weights)
    length = size_one * cols
    bins = np.arange(cols) - BLOCK // 2
    near = unit(np.arange(rows)[:, None] * bins[None, :] % length / length, 1.0 / math.sqrt(length))
    far = unit(np.arange(ranks)[:, None] * rows * bins[None, :] % length / length)
    count = kernels.shape[1]
    half = count // 2
    tall = rows + PAD
    hops = ranks // 2
    copies = pltpu.SemaphoreType.DMA
    marks = np.cumsum([0] + [len(x) for x in (*near, *far)]).tolist()
    constants = [first_waves(cols), np.concatenate((*near, *far)), second_waves(size_one)]
    operands = [samples, *(jnp.asarray(x) for x in constants), kernels, offsets, weight_index, level_weights]
    shapes = [pltpu.VMEM(x.shape, x.dtype) for x in operands[:5]] + [pltpu.SMEM(x.shape, x.dtype) for x in operands[5:]]
    power, got = pl.pallas_call(
        functools.partial(gather_kernel, marks),
        out_shape=(
            jax.ShapeDtypeStruct((count, segs, ranks, rows, BLOCK), BF16),
            jax.ShapeDtypeStruct((half, ranks, rows, BLOCK), BF16),
        ),
        in_specs=[pl.BlockSpec(memory_space=pltpu.HBM)] * len(operands),
        out_specs=(VMEM, VMEM),
        scratch_shapes=shapes
        + [
            pltpu.VMEM((segs * comps * rows, cols), BF16),
            pltpu.VMEM((16, cols), F32),
            pltpu.VMEM((segs * comps, rows, BLOCK), F32),
            pltpu.VMEM((ranks, RADIX, size_one // RADIX, segs * comps * BLOCK), BF16),
            pltpu.VMEM((segs, comps, ranks + 1, size_one + tall, BLOCK), BF16),
            pltpu.VMEM((count, 4 * BLOCK, 2 * BLOCK), BF16),
            pltpu.VMEM((2 * segs * tall, BLOCK), F32),
            pltpu.VMEM((half, ranks, rows, BLOCK), BF16),
        ]
        + [copies((7,)), copies((ranks,))]
        + [copies((2, ranks, hops))] * 2
        + [copies((half,))] * 2,
        compiler_params=pltpu.CompilerParams(vmem_limit_bytes=48 << 20, collective_id=0, has_side_effects=True),
    )(*(pltpu.with_memory_space_constraint(x, pltpu.HBM) for x in operands))
    out = pl.pallas_call(
        combine_kernel,
        out_shape=jax.ShapeDtypeStruct((half, rows, cols), F32),
        in_specs=[SMEM, VMEM, VMEM],
        out_specs=VMEM,
        compiler_params=pltpu.CompilerParams(vmem_limit_bytes=24 << 20),
    )(offsets, power, got)
    return out.reshape(half, rows * cols)


def solution(mesh):
    in_specs = (
        P(("parts", "seg"), None, "freq", None),
        P(),
        P(("parts", "seg"), None),
        P(("parts", "seg")),
        P(),
    )
    out_specs = P(("parts", "seg"), "freq")
    return jax.shard_map(body, mesh=mesh, in_specs=in_specs, out_specs=out_specs, check_vma=False)
```

```python
import math

import functools

import jax
import jax.numpy as jnp
import numpy as np
from jax import lax
from jax.experimental import pallas as pl
from jax.experimental.pallas import tpu as pltpu
from jax.sharding import PartitionSpec as P

BLOCK = 128
KERNELS = 8
REACH = 4
ROUTE_CAP = 4


def extended(cells, sides, width):
    for axis, dim in sides:
        count = lax.axis_size(axis)
        head = lax.slice_in_dim(cells, 0, width, axis=dim)
        tail = lax.slice_in_dim(cells, cells.shape[dim] - width, cells.shape[dim], axis=dim)
        cells = jnp.concatenate(
            [
                lax.ppermute(tail, axis, [(i, (i + 1) % count) for i in range(count)]),
                cells,
                lax.ppermute(head, axis, [((i + 1) % count, i) for i in range(count)]),
            ],
            axis=dim,
        )
    return cells


def passed_along(block, axis, distance):
    devices = range(lax.axis_size(axis))
    route = [((i - distance) % len(devices), i) for i in devices]
    return lax.ppermute(block, axis, route)


def dft_table(size):
    rows = lax.broadcasted_iota(jnp.int32, (size, size), 0)
    cols = lax.broadcasted_iota(jnp.int32, (size, size), 1)
    angle = (rows * cols % size).astype(jnp.float32) * (2.0 * math.pi / size)
    return (jnp.cos(angle), jnp.sin(angle))


def toeplitz(kernels):
    width = kernels.shape[-1]
    tail = jnp.zeros(kernels.shape[:-1] + (width + 1,), kernels.dtype)
    padded = jnp.concatenate([kernels, tail], -1)
    tiled = jnp.tile(padded, (1, 1, width))[..., : 2 * width * width]
    return tiled.reshape(kernels.shape[:-1] + (width, 2 * width))


def take_blocks(joined, start):
    return lax.dynamic_slice_in_dim(joined, start, joined.shape[0] // 2, 0)


def slide(joined, starts):
    return jax.vmap(jax.vmap(take_blocks))(joined, starts)


def general(samples, kernels, offsets, weight_index, level_weights):
    segs, comps, rows_one, cols_two = samples.shape
    ranks = lax.axis_size("freq")
    here = lax.axis_index("freq")
    size_one = rows_one * ranks
    length = size_one * cols_two
    highest = lax.Precision.HIGHEST
    cos_two, sin_two = dft_table(cols_two)
    stacked = samples.reshape(segs * comps * rows_one, cols_two)
    with_cos = jnp.dot(stacked, cos_two, precision=highest).reshape(samples.shape)
    with_sin = jnp.dot(stacked, sin_two, precision=highest).reshape(samples.shape)
    first_real = with_cos[:, 0] + with_sin[:, 1]
    first_imag = with_cos[:, 1] - with_sin[:, 0]
    row_global = here * rows_one + lax.broadcasted_iota(jnp.int32, (rows_one, cols_two), 0)
    col_global = lax.broadcasted_iota(jnp.int32, (rows_one, cols_two), 1)
    twist = (row_global * col_global % length).astype(jnp.float32) * (2.0 * math.pi / length)
    twist_cos = jnp.cos(twist)
    twist_sin = jnp.sin(twist)
    turned = jnp.stack(
        [
            first_real * twist_cos + first_imag * twist_sin,
            first_imag * twist_cos - first_real * twist_sin,
        ],
        1,
    )
    columns = lax.all_to_all(
        turned.astype(jnp.bfloat16), "freq", split_axis=3, concat_axis=3, tiled=True
    ).astype(turned.dtype)
    width_two = cols_two // ranks
    ordered = columns.reshape(segs, comps, rows_one, ranks, width_two)
    cos_one, sin_one = dft_table(size_one)
    cos_one = cos_one.reshape(ranks, rows_one, size_one)
    sin_one = sin_one.reshape(ranks, rows_one, size_one)
    second_cos = jnp.einsum("scirl,rik->sclk", ordered, cos_one, precision=highest)
    second_sin = jnp.einsum("scirl,rik->sclk", ordered, sin_one, precision=highest)
    second = jnp.stack(
        [second_cos[:, 0] + second_sin[:, 1], second_cos[:, 1] - second_sin[:, 0]], 1
    )
    arrived = lax.all_to_all(
        second.astype(jnp.bfloat16), "freq", split_axis=3, concat_axis=3, tiled=True
    ).astype(second.dtype)
    width_one = size_one // ranks
    spectrum = arrived.reshape(segs, comps, width_two, ranks, width_one)
    spectrum = jnp.transpose(spectrum, (0, 1, 4, 3, 2)).reshape(segs, comps, width_one * cols_two)
    spectrum = (spectrum * (1.0 / math.sqrt(length))).astype(jnp.bfloat16)
    half = BLOCK // 2
    edged = extended(spectrum, (("freq", 2),), half)
    bins_here = spectrum.shape[2]
    count = bins_here // BLOCK
    lower = edged[..., :bins_here].reshape(segs, comps, count, BLOCK)
    upper = edged[..., BLOCK:].reshape(segs, comps, count, BLOCK)
    window = jnp.concatenate([lower, upper], -1)
    bands = toeplitz(kernels)
    real_band = bands[0]
    imag_band = bands[1]
    table = jnp.stack(
        [jnp.stack([real_band, imag_band], 0), jnp.stack([-imag_band, real_band], 0)], 0
    )
    filtered = jnp.einsum("scbm,cokim->skboi", window, table, preferred_element_type=jnp.float32)
    power = (filtered[:, :, :, 0] ** 2 + filtered[:, :, :, 1] ** 2).astype(jnp.bfloat16)
    quotient = jnp.floor_divide(offsets, count)
    remainder = offsets - quotient * count
    following = passed_along(power, "freq", -1)
    inner = slide(jnp.concatenate([power, following], 2), remainder)
    plane_count = segs * KERNELS
    flat = inner.reshape(plane_count, count * BLOCK)
    plane_quot = quotient.reshape(plane_count)
    distances = lax.broadcasted_iota(jnp.int32, (2 * REACH + 1, plane_count), 0) - REACH
    member = (plane_quot[None, :] == distances).astype(jnp.int32)
    earlier = lax.broadcasted_iota(jnp.int32, (plane_count, plane_count), 0)
    later = lax.broadcasted_iota(jnp.int32, (plane_count, plane_count), 1)
    place = jnp.sum(jnp.where(earlier <= later, member[:, :, None], 0), 1) - 1
    slot_ids = lax.broadcasted_iota(jnp.int32, (2 * REACH + 1, ROUTE_CAP, plane_count), 1)
    select = ((member[:, None, :] == 1) & (place[:, None, :] == slot_ids)).astype(jnp.bfloat16)
    packed = jnp.einsum("dcp,pl->dcl", select, flat, preferred_element_type=jnp.float32).astype(
        jnp.bfloat16
    )
    received = []
    for step_index in range(2 * REACH + 1):
        received.append(passed_along(packed[step_index], "freq", -(step_index - REACH)))
    gathered = jnp.stack(received, 0)
    placed = jnp.einsum("dcp,dcl->pl", select, gathered, preferred_element_type=jnp.float32)
    shifted = placed.astype(jnp.bfloat16).reshape(segs, KERNELS, count, BLOCK)
    levels = lax.broadcasted_iota(jnp.int32, (segs, level_weights.shape[0]), 1)
    weights = jnp.sum(jnp.where(weight_index[:, None] == levels, level_weights[None, :], 0.0), 1)
    scale = 1.0 / (segs * lax.axis_size("seg"))
    partial_sum = jnp.sum((weights * scale)[:, None, None, None] * shifted.astype(jnp.float32), 0)
    owned = lax.psum_scatter(
        partial_sum.astype(jnp.bfloat16), "seg", scatter_dimension=0, tiled=True
    ).astype(jnp.float32)
    return owned.reshape(owned.shape[0], count * BLOCK)


VMEM = pl.BlockSpec(memory_space=pltpu.VMEM)
SMEM = pl.BlockSpec(memory_space=pltpu.SMEM)
PAD = 16
RADIX = 4
LEAD = 3
BF16 = jnp.bfloat16
F32 = jnp.float32


def unit(turns, scale=1.0):
    angle = 2.0 * np.pi * turns
    return (np.cos(angle) * scale).astype(np.float32), (np.sin(angle) * scale).astype(np.float32)


def first_waves(size):
    turns = np.arange(size)[:, None] * (np.arange(size) - BLOCK // 2)[None, :] % size / size
    both = np.stack([x.reshape(size, size // BLOCK, BLOCK) for x in unit(turns)], 2)
    return np.transpose(both, (1, 0, 2, 3)).reshape(size // BLOCK, size, 2 * BLOCK).astype(BF16)


def second_waves(size):
    quarter = size // RADIX
    places = np.arange(quarter)[None, None, :] * RADIX + np.arange(RADIX)[:, None, None]
    turns = np.arange(quarter)[None, :, None] * places % size / size
    return np.concatenate(unit(turns), 1).astype(BF16)


def fill_bands(taps_ref, band_ref):
    wide = 2 * BLOCK
    for t in range(taps_ref.shape[1]):
        both = []
        for c in range(2):
            row = taps_ref[c, t : t + 1, :].astype(F32)
            row = jnp.concatenate([row, jnp.zeros_like(row)], 1)
            row = jnp.broadcast_to(row, (BLOCK, wide))
            both.append(pltpu.roll(row, 0, 1, stride=1, stride_axis=0).T)
        re, im = both
        band_ref[t, :wide, :BLOCK] = re.astype(BF16)
        band_ref[t, :wide, BLOCK:] = im.astype(BF16)
        band_ref[t, wide:, :BLOCK] = (-im).astype(BF16)
        band_ref[t, wide:, BLOCK:] = re.astype(BF16)


def remote(src, dst, sems, at, axis, device):
    return pltpu.make_async_remote_copy(
        src_ref=src,
        dst_ref=dst,
        send_sem=sems[0].at[at],
        recv_sem=sems[1].at[at],
        device_id={axis: device},
        device_id_type=pl.DeviceIdType.MESH,
    )


def first_step(segs, rows, table_ref, xb_ref, near_ref, far_ref, mixed_ref, me, j):
    lanes = pl.ds(pl.multiple_of(j * BLOCK, BLOCK), BLOCK)
    got = jnp.dot(xb_ref[...], table_ref[j], preferred_element_type=F32)
    a = far_ref[me, 0:1, lanes]
    b = far_ref[me, 1:2, lanes]
    near_cos = near_ref[j, :rows]
    near_sin = near_ref[j, rows:]
    wc = a * near_cos - b * near_sin
    ws = b * near_cos + a * near_sin
    for s in range(segs):
        top = got[2 * s * rows : (2 * s + 1) * rows]
        low = got[(2 * s + 1) * rows : (2 * s + 2) * rows]
        re = top[:, :BLOCK] + low[:, BLOCK:]
        im = low[:, :BLOCK] - top[:, BLOCK:]
        mixed_ref[2 * s] = re * wc + im * ws
        mixed_ref[2 * s + 1] = im * wc - re * ws


def second_step(segs, wave_ref, turned_ref, w_ref, j):
    wide = 2 * BLOCK
    quarter = wave_ref.shape[1] // 2
    total = quarter * RADIX
    tall = w_ref.shape[3] - total
    for s in range(segs):
        terms = []
        for c in range(RADIX):
            y = jnp.dot(
                wave_ref[c], turned_ref[j, c, :, s * wide : (s + 1) * wide], preferred_element_type=F32
            )
            re = y[:quarter, :BLOCK] + y[quarter:, BLOCK:]
            im = y[:quarter, BLOCK:] - y[quarter:, :BLOCK]
            terms.append((re, im))
        (r0, i0), (r1, i1), (r2, i2), (r3, i3) = terms
        re = (r0 + r2) + (r1 + r3), (r0 - r2) + (i1 - i3), (r0 + r2) - (r1 + r3), (r0 - r2) - (i1 - i3)
        im = (i0 + i2) + (i1 + i3), (i0 - i2) - (r1 - r3), (i0 + i2) - (i1 + i3), (i0 - i2) + (r1 - r3)
        for m in range(RADIX):
            here = slice(m * quarter, (m + 1) * quarter)
            w_ref[s, 0, j, here, :] = re[m].astype(BF16)
            w_ref[s, 1, j, here, :] = im[m].astype(BF16)
        for c in range(2):
            w_ref[s, c, j, total:, :] = w_ref[s, c, j, :tall, :]


def wrap_column(w_ref, total):
    segs, comps, columns, high, _ = w_ref.shape
    for s in range(segs):
        for c in range(comps):
            x = w_ref[s, c, 0, :total, :].astype(F32)
            w_ref[s, c, columns - 1, :total, :] = jnp.concatenate([x[1:], x[:1]], 0).astype(BF16)
            w_ref[s, c, columns - 1, total:, :] = w_ref[s, c, columns - 1, : high - total, :]


def source_of(off_ref, s, t, total, ranks):
    blocks = total * ranks
    base = lax.rem(lax.axis_index("freq") * total + off_ref[s, t] + blocks, blocks)
    return base // ranks, lax.rem(base, ranks)


def filter_some(w_ref, band_ref, p_ref, power_ref, off_ref, weights, first, columns, rows, ranks, low, high):
    segs = len(weights)
    total = rows * ranks
    tall = rows + PAD
    count = band_ref.shape[0]

    @pl.loop(low, high, unroll=4)
    def _(i):
        t = lax.rem(first + i, count)
        parts = []
        shifts = []
        for s in range(segs):
            gk, gj = source_of(off_ref, s, t, total, ranks)
            for j in columns:
                row = lax.rem(gk + (gj - j + ranks - 1) // ranks, total)
                start = row // PAD * PAD
                shifts.append(row - start)
                take = pl.ds(start, tall)
                pieces = [w_ref[s, c, j + e, take, :] for c in range(2) for e in range(2)]
                parts.append(jnp.concatenate(pieces, 1))
        got = jnp.dot(jnp.concatenate(parts, 0), band_ref[t], preferred_element_type=F32)
        re = got[:, :BLOCK]
        im = got[:, BLOCK:]
        p_ref[...] = re * re + im * im
        for s in range(segs):
            for n, j in enumerate(columns):
                at = s * len(columns) + n
                x = p_ref[pl.ds(at * tall + shifts[at], rows), :]
                power_ref[i, s, j] = (weights[s] * x).astype(BF16)


def gather_kernel(
    x_hbm, first_hbm, near_hbm, far_hbm, wave_hbm, taps_hbm, off_hbm, wi_hbm, lw_hbm,
    power_ref, got_ref,
    x_ref, table_ref, near_ref, far_ref, wave_ref, taps_ref, off_ref, wi_ref, lw_ref,
    xb_ref, mixed_ref, turned_ref, w_ref, band_ref, p_ref, send_ref,
    in_sem,
    ring_send, ring_recv, core_send, core_recv,
):
    segs, comps, rows, cols = x_ref.shape
    ranks = lax.axis_size("freq")
    total = rows * ranks
    hops = ranks // 2
    part = rows // RADIX
    me = lax.axis_index("freq")
    core = lax.axis_index("seg")
    half = got_ref.shape[0]

    rest = slice(1, ranks)
    pairs = [
        (x_hbm.at[0], x_ref.at[0]), (x_hbm.at[1], x_ref.at[1]), (first_hbm.at[0], table_ref.at[0]),
        (near_hbm.at[0], near_ref.at[0]), (far_hbm, far_ref),
        (first_hbm.at[rest], table_ref.at[rest]), (near_hbm.at[rest], near_ref.at[rest]),
        (off_hbm, off_ref), (wi_hbm, wi_ref), (lw_hbm, lw_ref), (taps_hbm, taps_ref), (wave_hbm, wave_ref),
    ]
    fetches = [pltpu.make_async_copy(src, dst, in_sem.at[n]) for n, (src, dst) in enumerate(pairs)]
    for fetch in fetches[:7]:
        fetch.start()

    odd = me % 2
    place = (1 - odd) * (me // 2) + odd * (ranks - 1 - me // 2)

    def at_place(p):
        p = (p + ranks) % ranks
        far = p // (ranks // 2)
        return (1 - far) * (2 * p) + far * (2 * (ranks - 1 - p) + 1)

    barrier = pltpu.get_barrier_semaphore()
    for peer in (at_place(place + 1), at_place(place - 1)):
        pl.semaphore_signal(barrier, inc=1, device_id={"freq": peer}, device_id_type=pl.DeviceIdType.MESH)
    pl.semaphore_signal(barrier, inc=1, device_id={"seg": 1 - core}, device_id_type=pl.DeviceIdType.MESH)

    def moved(j, k, way, origin):
        owner = at_place(place - origin) if way == 0 else at_place(place + origin)
        target = at_place(place + 1) if way == 0 else at_place(place - 1)
        classes = pl.ds(0, RADIX) if k < hops - 1 else pl.ds(way * (RADIX // 2), RADIX // 2)
        block = turned_ref.at[j, classes, pl.ds(pl.multiple_of(owner * part, part), part), :]
        return remote(block, block, (ring_send, ring_recv), (way, j, k), "freq", target)

    def send(j, k):
        for way in range(2):
            moved(j, k, way, k).start()

    def landed(j, k):
        for way in range(2):
            moved(j, k, way, k + 1).wait_recv()

    own_rows = pl.ds(pl.multiple_of(me * part, part), part)
    for s in range(segs):
        fetches[s].wait()
        for c in range(comps):
            at = (s * comps + c) * rows
            xb_ref[at : at + rows, :] = x_ref[s, c].astype(BF16)
    for fetch in fetches[2:5]:
        fetch.wait()
    for fetch in fetches[7:]:
        fetch.start()

    @pl.loop(0, ranks)
    def _(j):
        @pl.when(j == 1)
        def _():
            for fetch in fetches[5:7]:
                fetch.wait()

        first_step(segs, rows, table_ref, xb_ref, near_ref, far_ref, mixed_ref, me, j)
        for n in range(RADIX):
            for i in range(segs * comps):
                lanes = slice(i * BLOCK, (i + 1) * BLOCK)
                turned_ref[j, n, own_rows, lanes] = mixed_ref[i, pl.ds(n, part, stride=RADIX), :].astype(BF16)

        @pl.when(j == 0)
        def _():
            pl.semaphore_wait(barrier, 3)

        @pl.when(j < LEAD)
        def _():
            send(j, 0)

    for fetch in fetches[7:]:
        fetch.wait()
    weights = [lw_ref[wi_ref[s]] * (1.0 / (2 * segs)) for s in range(segs)]
    sift = functools.partial(filter_some, w_ref, band_ref, p_ref, power_ref, off_ref, weights, core * half)

    @pl.loop(0, ranks + hops - 1)
    def _(q):
        @pl.when(q < ranks)
        def _():
            landed(q, 0)
            send(q, 1)

        @pl.when(q < ranks - LEAD)
        def _():
            send(q + LEAD, 0)

        @pl.when(q == 0)
        def _():
            fill_bands(taps_ref, band_ref)

        for k in range(1, hops - 1):

            @pl.when((q >= k) & (q < ranks + k))
            def _():
                landed(q - k, k)
                send(q - k, k + 1)

        for pair in range(ranks // 2 - 1):

            @pl.when(q == 2 * pair + hops + 2)
            def _():
                sift((2 * pair, 2 * pair + 1), rows, ranks, 0, 2 * half)

        @pl.when(q >= hops - 1)
        def _():
            landed(q - hops + 1, hops - 1)
            second_step(segs, wave_ref, turned_ref, w_ref, q - hops + 1)

        @pl.when(q == hops - 1)
        def _():
            wrap_column(w_ref, total)

    def swap(i):
        return remote(send_ref.at[i], got_ref.at[i], (core_send, core_recv), (i,), "seg", 1 - core)

    sift((ranks - 2, ranks - 1), rows, ranks, half, 2 * half)

    @pl.loop(0, half)
    def _(i):
        t = (1 - core) * half + i
        turns = [source_of(off_ref, s, t, total, ranks)[1] for s in range(segs)]
        for jj in range(ranks):
            x = sum(power_ref[half + i, s, lax.rem(turns[s] + jj, ranks)].astype(F32) for s in range(segs))
            send_ref[i, jj] = x.astype(BF16)
        swap(i).start()

    sift((ranks - 2, ranks - 1), rows, ranks, 0, half)

    @pl.loop(0, half)
    def _(i):
        swap(i).wait()

    @pl.loop(0, ranks)
    def _(j):
        for k in range(hops):
            for way in range(2):
                moved(j, k, way, k).wait_send()


def combine_kernel(off_ref, power_ref, got_ref, out_ref):
    half, ranks, rows, _ = got_ref.shape
    segs = power_ref.shape[1]
    core = lax.axis_index("seg")

    @pl.loop(0, half)
    def _(i):
        turns = [source_of(off_ref, s, core * half + i, rows * ranks, ranks)[1] for s in range(segs)]
        for jj in range(ranks):
            x = got_ref[i, jj].astype(F32)
            for s in range(segs):
                x = x + power_ref[i, s, lax.rem(turns[s] + jj, ranks)].astype(F32)
            out_ref[i, :, jj * BLOCK : (jj + 1) * BLOCK] = x


def body(samples, kernels, offsets, weight_index, level_weights):
    segs, comps, rows, cols = samples.shape
    ranks = lax.axis_size("freq")
    size_one = rows * ranks
    if cols != ranks * BLOCK or rows != BLOCK or size_one != cols or segs != 2 or lax.axis_size("seg") != 2:
        return general(samples, kernels, offsets, weight_index, level_weights)
    length = size_one * cols
    bins = np.arange(cols) - BLOCK // 2
    near = unit(np.arange(rows)[:, None] * bins[None, :] % length / length, 1.0 / math.sqrt(length))
    far = unit(np.arange(ranks)[:, None] * rows * bins[None, :] % length / length)
    count = kernels.shape[1]
    half = count // 2
    tall = rows + PAD
    hops = ranks // 2
    copies = pltpu.SemaphoreType.DMA
    near = np.transpose(np.concatenate(near).reshape(2 * rows, ranks, BLOCK), (1, 0, 2))
    constants = [first_waves(cols), near, np.stack(far, 1), second_waves(size_one)]
    operands = [samples, *(jnp.asarray(x) for x in constants), kernels, offsets, weight_index, level_weights]
    shapes = [pltpu.VMEM(x.shape, x.dtype) for x in operands[:6]] + [pltpu.SMEM(x.shape, x.dtype) for x in operands[6:]]
    power, got = pl.pallas_call(
        gather_kernel,
        out_shape=(
            jax.ShapeDtypeStruct((count, segs, ranks, rows, BLOCK), BF16),
            jax.ShapeDtypeStruct((half, ranks, rows, BLOCK), BF16),
        ),
        in_specs=[pl.BlockSpec(memory_space=pltpu.HBM)] * len(operands),
        out_specs=(VMEM, VMEM),
        scratch_shapes=shapes
        + [
            pltpu.VMEM((segs * comps * rows, cols), BF16),
            pltpu.VMEM((segs * comps, rows, BLOCK), F32),
            pltpu.VMEM((ranks, RADIX, size_one // RADIX, segs * comps * BLOCK), BF16),
            pltpu.VMEM((segs, comps, ranks + 1, size_one + tall, BLOCK), BF16),
            pltpu.VMEM((count, 4 * BLOCK, 2 * BLOCK), BF16),
            pltpu.VMEM((2 * segs * tall, BLOCK), F32),
            pltpu.VMEM((half, ranks, rows, BLOCK), BF16),
        ]
        + [copies((12,))]
        + [copies((2, ranks, hops))] * 2
        + [copies((half,))] * 2,
        compiler_params=pltpu.CompilerParams(vmem_limit_bytes=48 << 20, collective_id=0, has_side_effects=True),
    )(*(pltpu.with_memory_space_constraint(x, pltpu.HBM) for x in operands))
    out = pl.pallas_call(
        combine_kernel,
        out_shape=jax.ShapeDtypeStruct((half, rows, cols), F32),
        in_specs=[SMEM, VMEM, VMEM],
        out_specs=VMEM,
        compiler_params=pltpu.CompilerParams(vmem_limit_bytes=24 << 20),
    )(offsets, power, got)
    return out.reshape(half, rows * cols)


def solution(mesh):
    in_specs = (
        P(("parts", "seg"), None, "freq", None),
        P(),
        P(("parts", "seg"), None),
        P(("parts", "seg")),
        P(),
    )
    out_specs = P(("parts", "seg"), "freq")
    return jax.shard_map(body, mesh=mesh, in_specs=in_specs, out_specs=out_specs, check_vma=False)
```

```python
import math

import functools

import jax
import jax.numpy as jnp
import numpy as np
from jax import lax
from jax.experimental import pallas as pl
from jax.experimental.pallas import tpu as pltpu
from jax.sharding import PartitionSpec as P

BLOCK = 128
KERNELS = 8
REACH = 4
ROUTE_CAP = 4


def extended(cells, sides, width):
    for axis, dim in sides:
        count = lax.axis_size(axis)
        head = lax.slice_in_dim(cells, 0, width, axis=dim)
        tail = lax.slice_in_dim(cells, cells.shape[dim] - width, cells.shape[dim], axis=dim)
        cells = jnp.concatenate(
            [
                lax.ppermute(tail, axis, [(i, (i + 1) % count) for i in range(count)]),
                cells,
                lax.ppermute(head, axis, [((i + 1) % count, i) for i in range(count)]),
            ],
            axis=dim,
        )
    return cells


def passed_along(block, axis, distance):
    devices = range(lax.axis_size(axis))
    route = [((i - distance) % len(devices), i) for i in devices]
    return lax.ppermute(block, axis, route)


def dft_table(size):
    rows = lax.broadcasted_iota(jnp.int32, (size, size), 0)
    cols = lax.broadcasted_iota(jnp.int32, (size, size), 1)
    angle = (rows * cols % size).astype(jnp.float32) * (2.0 * math.pi / size)
    return (jnp.cos(angle), jnp.sin(angle))


def toeplitz(kernels):
    width = kernels.shape[-1]
    tail = jnp.zeros(kernels.shape[:-1] + (width + 1,), kernels.dtype)
    padded = jnp.concatenate([kernels, tail], -1)
    tiled = jnp.tile(padded, (1, 1, width))[..., : 2 * width * width]
    return tiled.reshape(kernels.shape[:-1] + (width, 2 * width))


def take_blocks(joined, start):
    return lax.dynamic_slice_in_dim(joined, start, joined.shape[0] // 2, 0)


def slide(joined, starts):
    return jax.vmap(jax.vmap(take_blocks))(joined, starts)


def general(samples, kernels, offsets, weight_index, level_weights):
    segs, comps, rows_one, cols_two = samples.shape
    ranks = lax.axis_size("freq")
    here = lax.axis_index("freq")
    size_one = rows_one * ranks
    length = size_one * cols_two
    highest = lax.Precision.HIGHEST
    cos_two, sin_two = dft_table(cols_two)
    stacked = samples.reshape(segs * comps * rows_one, cols_two)
    with_cos = jnp.dot(stacked, cos_two, precision=highest).reshape(samples.shape)
    with_sin = jnp.dot(stacked, sin_two, precision=highest).reshape(samples.shape)
    first_real = with_cos[:, 0] + with_sin[:, 1]
    first_imag = with_cos[:, 1] - with_sin[:, 0]
    row_global = here * rows_one + lax.broadcasted_iota(jnp.int32, (rows_one, cols_two), 0)
    col_global = lax.broadcasted_iota(jnp.int32, (rows_one, cols_two), 1)
    twist = (row_global * col_global % length).astype(jnp.float32) * (2.0 * math.pi / length)
    twist_cos = jnp.cos(twist)
    twist_sin = jnp.sin(twist)
    turned = jnp.stack(
        [
            first_real * twist_cos + first_imag * twist_sin,
            first_imag * twist_cos - first_real * twist_sin,
        ],
        1,
    )
    columns = lax.all_to_all(
        turned.astype(jnp.bfloat16), "freq", split_axis=3, concat_axis=3, tiled=True
    ).astype(turned.dtype)
    width_two = cols_two // ranks
    ordered = columns.reshape(segs, comps, rows_one, ranks, width_two)
    cos_one, sin_one = dft_table(size_one)
    cos_one = cos_one.reshape(ranks, rows_one, size_one)
    sin_one = sin_one.reshape(ranks, rows_one, size_one)
    second_cos = jnp.einsum("scirl,rik->sclk", ordered, cos_one, precision=highest)
    second_sin = jnp.einsum("scirl,rik->sclk", ordered, sin_one, precision=highest)
    second = jnp.stack(
        [second_cos[:, 0] + second_sin[:, 1], second_cos[:, 1] - second_sin[:, 0]], 1
    )
    arrived = lax.all_to_all(
        second.astype(jnp.bfloat16), "freq", split_axis=3, concat_axis=3, tiled=True
    ).astype(second.dtype)
    width_one = size_one // ranks
    spectrum = arrived.reshape(segs, comps, width_two, ranks, width_one)
    spectrum = jnp.transpose(spectrum, (0, 1, 4, 3, 2)).reshape(segs, comps, width_one * cols_two)
    spectrum = (spectrum * (1.0 / math.sqrt(length))).astype(jnp.bfloat16)
    half = BLOCK // 2
    edged = extended(spectrum, (("freq", 2),), half)
    bins_here = spectrum.shape[2]
    count = bins_here // BLOCK
    lower = edged[..., :bins_here].reshape(segs, comps, count, BLOCK)
    upper = edged[..., BLOCK:].reshape(segs, comps, count, BLOCK)
    window = jnp.concatenate([lower, upper], -1)
    bands = toeplitz(kernels)
    real_band = bands[0]
    imag_band = bands[1]
    table = jnp.stack(
        [jnp.stack([real_band, imag_band], 0), jnp.stack([-imag_band, real_band], 0)], 0
    )
    filtered = jnp.einsum("scbm,cokim->skboi", window, table, preferred_element_type=jnp.float32)
    power = (filtered[:, :, :, 0] ** 2 + filtered[:, :, :, 1] ** 2).astype(jnp.bfloat16)
    quotient = jnp.floor_divide(offsets, count)
    remainder = offsets - quotient * count
    following = passed_along(power, "freq", -1)
    inner = slide(jnp.concatenate([power, following], 2), remainder)
    plane_count = segs * KERNELS
    flat = inner.reshape(plane_count, count * BLOCK)
    plane_quot = quotient.reshape(plane_count)
    distances = lax.broadcasted_iota(jnp.int32, (2 * REACH + 1, plane_count), 0) - REACH
    member = (plane_quot[None, :] == distances).astype(jnp.int32)
    earlier = lax.broadcasted_iota(jnp.int32, (plane_count, plane_count), 0)
    later = lax.broadcasted_iota(jnp.int32, (plane_count, plane_count), 1)
    place = jnp.sum(jnp.where(earlier <= later, member[:, :, None], 0), 1) - 1
    slot_ids = lax.broadcasted_iota(jnp.int32, (2 * REACH + 1, ROUTE_CAP, plane_count), 1)
    select = ((member[:, None, :] == 1) & (place[:, None, :] == slot_ids)).astype(jnp.bfloat16)
    packed = jnp.einsum("dcp,pl->dcl", select, flat, preferred_element_type=jnp.float32).astype(
        jnp.bfloat16
    )
    received = []
    for step_index in range(2 * REACH + 1):
        received.append(passed_along(packed[step_index], "freq", -(step_index - REACH)))
    gathered = jnp.stack(received, 0)
    placed = jnp.einsum("dcp,dcl->pl", select, gathered, preferred_element_type=jnp.float32)
    shifted = placed.astype(jnp.bfloat16).reshape(segs, KERNELS, count, BLOCK)
    levels = lax.broadcasted_iota(jnp.int32, (segs, level_weights.shape[0]), 1)
    weights = jnp.sum(jnp.where(weight_index[:, None] == levels, level_weights[None, :], 0.0), 1)
    scale = 1.0 / (segs * lax.axis_size("seg"))
    partial_sum = jnp.sum((weights * scale)[:, None, None, None] * shifted.astype(jnp.float32), 0)
    owned = lax.psum_scatter(
        partial_sum.astype(jnp.bfloat16), "seg", scatter_dimension=0, tiled=True
    ).astype(jnp.float32)
    return owned.reshape(owned.shape[0], count * BLOCK)


VMEM = pl.BlockSpec(memory_space=pltpu.VMEM)
SMEM = pl.BlockSpec(memory_space=pltpu.SMEM)
PAD = 16
RADIX = 4
LAG = 4
BF16 = jnp.bfloat16
F32 = jnp.float32


def unit(turns, scale=1.0):
    angle = 2.0 * np.pi * turns
    return (np.cos(angle) * scale).astype(np.float32), (np.sin(angle) * scale).astype(np.float32)


def first_waves(size):
    turns = np.arange(size)[:, None] * (np.arange(size) - BLOCK // 2)[None, :] % size / size
    both = np.stack([x.reshape(size, size // BLOCK, BLOCK) for x in unit(turns)], 2)
    return np.transpose(both, (1, 0, 2, 3)).reshape(size // BLOCK, size, 2 * BLOCK).astype(BF16)


def second_waves(size):
    quarter = size // RADIX
    places = np.arange(quarter)[None, None, :] * RADIX + np.arange(RADIX)[:, None, None]
    turns = np.arange(quarter)[None, :, None] * places % size / size
    return np.concatenate(unit(turns), 1).astype(BF16)


def fill_bands(taps_ref, band_ref):
    wide = 2 * BLOCK
    for t in range(taps_ref.shape[1]):
        both = []
        for c in range(2):
            row = taps_ref[c, t : t + 1, :].astype(F32)
            row = jnp.concatenate([row, jnp.zeros_like(row)], 1)
            row = jnp.broadcast_to(row, (BLOCK, wide))
            both.append(pltpu.roll(row, 0, 1, stride=1, stride_axis=0).T)
        re, im = both
        band_ref[t, :wide, :BLOCK] = re.astype(BF16)
        band_ref[t, :wide, BLOCK:] = im.astype(BF16)
        band_ref[t, wide:, :BLOCK] = (-im).astype(BF16)
        band_ref[t, wide:, BLOCK:] = re.astype(BF16)


def remote(src, dst, sems, at, device):
    return pltpu.make_async_remote_copy(
        src_ref=src,
        dst_ref=dst,
        send_sem=sems[0].at[at],
        recv_sem=sems[1].at[at],
        device_id=device,
        device_id_type=pl.DeviceIdType.MESH,
    )


def first_step(segs, rows, table_ref, xb_ref, near_ref, far_ref, mixed_ref, me, j):
    lanes = pl.ds(pl.multiple_of(j * BLOCK, BLOCK), BLOCK)
    got = jnp.dot(xb_ref[...], table_ref[j], preferred_element_type=F32)
    a = far_ref[me, 0:1, lanes]
    b = far_ref[me, 1:2, lanes]
    near_cos = near_ref[j, :rows]
    near_sin = near_ref[j, rows:]
    wc = a * near_cos - b * near_sin
    ws = b * near_cos + a * near_sin
    for s in range(segs):
        top = got[2 * s * rows : (2 * s + 1) * rows]
        low = got[(2 * s + 1) * rows : (2 * s + 2) * rows]
        re = top[:, :BLOCK] + low[:, BLOCK:]
        im = low[:, :BLOCK] - top[:, BLOCK:]
        mixed_ref[2 * s] = re * wc + im * ws
        mixed_ref[2 * s + 1] = im * wc - re * ws


def second_step(wave_ref, turned_ref, w_ref, j):
    quarter = wave_ref.shape[1] // 2
    total = quarter * RADIX
    tall = w_ref.shape[2] - total
    terms = []
    for c in range(RADIX):
        y = jnp.dot(wave_ref[c], turned_ref[j, c], preferred_element_type=F32)
        re = y[:quarter, :BLOCK] + y[quarter:, BLOCK:]
        im = y[:quarter, BLOCK:] - y[quarter:, :BLOCK]
        terms.append((re, im))
    (r0, i0), (r1, i1), (r2, i2), (r3, i3) = terms
    re = (r0 + r2) + (r1 + r3), (r0 - r2) + (i1 - i3), (r0 + r2) - (r1 + r3), (r0 - r2) - (i1 - i3)
    im = (i0 + i2) + (i1 + i3), (i0 - i2) - (r1 - r3), (i0 + i2) - (i1 + i3), (i0 - i2) + (r1 - r3)
    for m in range(RADIX):
        here = slice(m * quarter, (m + 1) * quarter)
        w_ref[0, j, here, :] = re[m].astype(BF16)
        w_ref[1, j, here, :] = im[m].astype(BF16)
    for c in range(2):
        w_ref[c, j, total:, :] = w_ref[c, j, :tall, :]


def wrap_column(w_ref, total):
    comps, columns, high, _ = w_ref.shape
    for c in range(comps):
        x = w_ref[c, 0, :total, :].astype(F32)
        w_ref[c, columns - 1, :total, :] = jnp.concatenate([x[1:], x[:1]], 0).astype(BF16)
        w_ref[c, columns - 1, total:, :] = w_ref[c, columns - 1, : high - total, :]


def source_of(first, offset, total, ranks):
    blocks = total * ranks
    base = lax.rem(first * total + offset + blocks, blocks)
    return base // ranks, lax.rem(base, ranks)


def filter_some(w_ref, band_ref, p_ref, off_ref, weight, first, columns, rows, ranks, stores):
    total = rows * ranks
    tall = 2 * rows + PAD
    half = band_ref.shape[0] // 2
    me = lax.axis_index("freq")
    side = me % 2

    @pl.loop(0, half, unroll=half)
    def _(i):
        t = first + i
        gk, gj = source_of(me - side, off_ref[side, t], total, ranks)
        parts = []
        shifts = []
        for j in columns:
            row = lax.rem(gk + (gj - j + ranks - 1) // ranks, total)
            start = row // PAD * PAD
            shifts.append(row - start)
            take = pl.ds(start, tall)
            pieces = [w_ref[c, j + e, take, :] for c in range(2) for e in range(2)]
            parts.append(jnp.concatenate(pieces, 1))
        got = jnp.dot(jnp.concatenate(parts, 0), band_ref[t], preferred_element_type=F32)
        re = got[:, :BLOCK]
        im = got[:, BLOCK:]
        p_ref[i] = re * re + im * im
        for n, j in enumerate(columns):
            for which, store in ((1 - side, stores[0]), (side, stores[1])):
                x = p_ref[i, pl.ds(n * tall + shifts[n] + which * rows, rows), :]
                store(i, j, (weight * x).astype(BF16))


def gather_kernel(
    x_hbm, first_hbm, near_hbm, far_hbm, wave_hbm, taps_hbm, off_hbm, wi_hbm, lw_hbm,
    in_ref,
    x_ref, table_ref, near_ref, far_ref, wave_ref, taps_ref, off_ref, wi_ref, lw_ref,
    xb_ref, mixed_ref, turned_ref, other_ref, w_ref, band_ref, p_ref, away_ref, core_ref,
    in_sem, pair_send, pair_recv, line_send, line_recv, out_send, out_recv, go_sem,
):
    segs, comps, rows, cols = x_ref.shape
    ranks = lax.axis_size("freq")
    total = rows * ranks
    planes = ranks // 2
    part = rows // RADIX
    me = lax.axis_index("freq")
    core = lax.axis_index("seg")
    side = me % 2
    plane = me // 2
    pair = me + 1 - 2 * side
    half = in_ref.shape[1]

    rest = slice(1, ranks)
    pairs = [
        (x_hbm.at[0], x_ref.at[0]), (x_hbm.at[1], x_ref.at[1]), (first_hbm.at[0], table_ref.at[0]),
        (near_hbm.at[0], near_ref.at[0]), (far_hbm, far_ref),
        (first_hbm.at[rest], table_ref.at[rest]), (near_hbm.at[rest], near_ref.at[rest]),
        (off_hbm, off_ref), (wi_hbm, wi_ref), (lw_hbm, lw_ref), (taps_hbm, taps_ref), (wave_hbm, wave_ref),
    ]
    fetches = [pltpu.make_async_copy(src, dst, in_sem.at[n]) for n, (src, dst) in enumerate(pairs)]
    for fetch in fetches[:7]:
        fetch.start()

    barrier = pltpu.get_barrier_semaphore()

    def greet(device):
        pl.semaphore_signal(barrier, inc=1, device_id=device, device_id_type=pl.DeviceIdType.MESH)

    greet({"seg": 1 - core})
    greet({"freq": pair})
    greet({"freq": pair, "seg": 1 - core})

    @pl.when(plane > 0)
    def _():
        greet({"freq": me - 2})

    @pl.when(plane < planes - 1)
    def _():
        greet({"freq": me + 2})

    def crossed(j, owner):
        place = turned_ref.at[j, :, pl.ds(pl.multiple_of(owner * part, part), part), :]
        return remote(other_ref.at[j], place, (pair_send, pair_recv), (j,), {"freq": pair})

    def moved(j, k, way, origin):
        rows_at = pl.ds(pl.multiple_of(origin * (2 * part), 2 * part), 2 * part)
        block = turned_ref.at[j, :, rows_at, :]
        target = me + 2 if way == 0 else me - 2
        return remote(block, block, (line_send, line_recv), (way, j, k), {"freq": target})

    def each_sent(j, k, act):
        @pl.when((plane < planes - 1) & (plane >= k))
        def _():
            act(moved(j, k, 0, plane - k))

        @pl.when((plane > 0) & (plane <= planes - 1 - k))
        def _():
            act(moved(j, k, 1, plane + k))

    def send(j, k):
        each_sent(j, k, lambda copy: copy.start())

    def landed(j, k):
        @pl.when(plane >= k + 1)
        def _():
            moved(j, k, 0, plane - 1 - k).wait_recv()

        @pl.when(plane <= planes - 2 - k)
        def _():
            moved(j, k, 1, plane + 1 + k).wait_recv()

    own_rows = pl.ds(pl.multiple_of(me * part, part), part)
    for s in range(segs):
        fetches[s].wait()
        for c in range(comps):
            at = (s * comps + c) * rows
            xb_ref[at : at + rows, :] = x_ref[s, c].astype(BF16)
    for fetch in fetches[2:5]:
        fetch.wait()
    for fetch in fetches[7:]:
        fetch.start()

    @pl.loop(0, ranks)
    def _(j):
        @pl.when(j == 1)
        def _():
            for fetch in fetches[5:7]:
                fetch.wait()

        first_step(segs, rows, table_ref, xb_ref, near_ref, far_ref, mixed_ref, me, j)
        for n in range(RADIX):
            for i in range(comps):
                lanes = slice(i * BLOCK, (i + 1) * BLOCK)
                take = pl.ds(n, part, stride=RADIX)
                other_ref[j, n, :, lanes] = mixed_ref[2 * (1 - side) + i, take, :].astype(BF16)
                turned_ref[j, n, own_rows, lanes] = mixed_ref[2 * side + i, take, :].astype(BF16)

        @pl.when(j == 0)
        def _():
            below = (plane + planes - 1) // planes
            above = (2 * planes - 2 - plane) // planes
            pl.semaphore_wait(barrier, 3 + below + above)

        crossed(j, me).start()

    for fetch in fetches[7:]:
        fetch.wait()
    weight = lw_ref[wi_ref[side]] * (1.0 / (2 * segs))
    here = 2 * side + core

    def keep(ref, *lead):
        def store(i, j, x):
            ref[(*lead, i, j)] = x

        return store

    def leave(kind, stage):
        take = pl.ds(2 * stage, 2)
        src = core_ref.at[:, take] if kind == 2 else away_ref.at[kind, :, take]
        device = ({"freq": pair}, {"freq": pair, "seg": 1 - core}, {"seg": 1 - core})[kind]
        return remote(src, in_ref.at[here, :, take], (out_send, out_recv), (kind, stage), device)

    def arrive(kind, stage):
        source = (2 * (1 - side) + core, 2 * (1 - side) + 1 - core, 2 * side + 1 - core)[kind]
        take = pl.ds(2 * stage, 2)
        src = core_ref.at[:, take] if kind == 2 else away_ref.at[kind, :, take]
        device = ({"freq": pair}, {"freq": pair, "seg": 1 - core}, {"seg": 1 - core})[kind]
        return remote(src, in_ref.at[source, :, take], (out_send, out_recv), (kind, stage), device)

    def sift(stage):
        columns = (2 * stage, 2 * stage + 1)
        run = functools.partial(filter_some, w_ref, band_ref, p_ref, off_ref, weight)
        run((1 - core) * half, columns, rows, ranks, (keep(away_ref, 1), keep(core_ref)))
        leave(1, stage).start()
        leave(2, stage).start()
        run(core * half, columns, rows, ranks, (keep(away_ref, 0), keep(in_ref, here)))
        leave(0, stage).start()

    rounds = ranks + planes - 1

    @pl.when(core == 1)
    def _():
        pl.semaphore_wait(go_sem, LAG)

    @pl.loop(0, rounds)
    def _(q):
        @pl.when((core == 1) & (q < rounds - LAG))
        def _():
            pl.semaphore_wait(go_sem, 1)

        @pl.when(q < ranks)
        def _():
            crossed(q, pair).wait_recv()
            send(q, 0)

        for k in range(planes - 2):

            @pl.when((q > k) & (q <= ranks + k))
            def _():
                landed(q - k - 1, k)
                send(q - k - 1, k + 1)

        @pl.when(core == 0)
        def _():
            pl.semaphore_signal(go_sem, inc=1, device_id={"seg": 1 - core}, device_id_type=pl.DeviceIdType.MESH)

        @pl.when(q == 0)
        def _():
            fill_bands(taps_ref, band_ref)

        @pl.when(q >= planes - 1)
        def _():
            landed(q - planes + 1, planes - 2)
            second_step(wave_ref, turned_ref, w_ref, q - planes + 1)

        @pl.when(q == planes - 1)
        def _():
            wrap_column(w_ref, total)

        for stage in range(planes - 1):

            @pl.when(q == 2 * stage + 2 + planes - 1)
            def _():
                sift(stage)

    sift(planes - 1)

    for stage in range(planes):
        for kind in range(3):
            arrive(kind, stage).wait_recv()

    @pl.loop(0, ranks)
    def _(j):
        crossed(j, me).wait_send()
        for k in range(planes - 1):
            each_sent(j, k, lambda copy: copy.wait_send())

    for stage in range(planes):
        for kind in range(3):
            leave(kind, stage).wait_send()


def combine_kernel(off_ref, far_off_ref, in_ref, out_ref):
    sources, half, ranks, rows, _ = in_ref.shape
    core = lax.axis_index("seg")
    me = lax.axis_index("freq")

    @pl.loop(0, half)
    def _(i):
        t = core * half + i
        places = []
        for side in range(2):
            for ref, where in ((off_ref, core), (far_off_ref, 1 - core)):
                places.append((2 * side + where, source_of(me, ref[side, t], rows * ranks, ranks)[1]))
        for jj in range(ranks):
            x = sum(in_ref[n, i, lax.rem(turn + jj, ranks)].astype(F32) for n, turn in places)
            out_ref[i, :, jj * BLOCK : (jj + 1) * BLOCK] = x


def body(samples, kernels, offsets, weight_index, level_weights):
    segs, comps, rows, cols = samples.shape
    ranks = lax.axis_size("freq")
    size_one = rows * ranks
    if cols != ranks * BLOCK or rows != BLOCK or size_one != cols or segs != 2 or lax.axis_size("seg") != 2:
        return general(samples, kernels, offsets, weight_index, level_weights)
    length = size_one * cols
    bins = np.arange(cols) - BLOCK // 2
    near = unit(np.arange(rows)[:, None] * bins[None, :] % length / length, 1.0 / math.sqrt(length))
    far = unit(np.arange(ranks)[:, None] * rows * bins[None, :] % length / length)
    count = kernels.shape[1]
    half = count // 2
    tall = 2 * rows + PAD
    planes = ranks // 2
    copies = pltpu.SemaphoreType.DMA
    near = np.transpose(np.concatenate(near).reshape(2 * rows, ranks, BLOCK), (1, 0, 2))
    constants = [first_waves(cols), near, np.stack(far, 1), second_waves(size_one)]
    operands = [samples, *(jnp.asarray(x) for x in constants), kernels, offsets, weight_index, level_weights]
    shapes = [pltpu.VMEM(x.shape, x.dtype) for x in operands[:6]] + [pltpu.SMEM(x.shape, x.dtype) for x in operands[6:]]
    far_offsets = lax.ppermute(offsets, "seg", [(0, 1), (1, 0)])
    power = pl.pallas_call(
        gather_kernel,
        out_shape=jax.ShapeDtypeStruct((4, half, ranks, rows, BLOCK), BF16),
        in_specs=[pl.BlockSpec(memory_space=pltpu.HBM)] * len(operands),
        out_specs=VMEM,
        scratch_shapes=shapes
        + [
            pltpu.VMEM((segs * comps * rows, cols), BF16),
            pltpu.VMEM((segs * comps, rows, BLOCK), F32),
            pltpu.VMEM((ranks, RADIX, size_one // RADIX, comps * BLOCK), BF16),
            pltpu.VMEM((ranks, RADIX, rows // RADIX, comps * BLOCK), BF16),
            pltpu.VMEM((comps, ranks + 1, size_one + tall, BLOCK), BF16),
            pltpu.VMEM((count, 4 * BLOCK, 2 * BLOCK), BF16),
            pltpu.VMEM((half, 2 * tall, BLOCK), F32),
            pltpu.VMEM((2, half, ranks, rows, BLOCK), BF16),
            pltpu.VMEM((half, ranks, rows, BLOCK), BF16),
        ]
        + [copies((12,))]
        + [copies((ranks,))] * 2
        + [copies((2, ranks, planes - 1))] * 2
        + [copies((3, planes))] * 2
        + [pltpu.SemaphoreType.REGULAR],
        compiler_params=pltpu.CompilerParams(vmem_limit_bytes=48 << 20, collective_id=0, has_side_effects=True),
    )(*(pltpu.with_memory_space_constraint(x, pltpu.HBM) for x in operands))
    out = pl.pallas_call(
        combine_kernel,
        out_shape=jax.ShapeDtypeStruct((half, rows, cols), F32),
        in_specs=[SMEM, SMEM, VMEM],
        out_specs=VMEM,
        compiler_params=pltpu.CompilerParams(vmem_limit_bytes=24 << 20),
    )(offsets, far_offsets, power)
    return out.reshape(half, rows * cols)


def solution(mesh):
    in_specs = (
        P(("parts", "seg"), None, "freq", None),
        P(),
        P(("parts", "seg"), None),
        P(("parts", "seg")),
        P(),
    )
    out_specs = P(("parts", "seg"), "freq")
    return jax.shard_map(body, mesh=mesh, in_specs=in_specs, out_specs=out_specs, check_vma=False)
```

```python
import math

import functools

import jax
import jax.numpy as jnp
import numpy as np
from jax import lax
from jax.experimental import pallas as pl
from jax.experimental.pallas import tpu as pltpu
from jax.sharding import PartitionSpec as P

BLOCK = 128
KERNELS = 8
REACH = 4
ROUTE_CAP = 4


def extended(cells, sides, width):
    for axis, dim in sides:
        count = lax.axis_size(axis)
        head = lax.slice_in_dim(cells, 0, width, axis=dim)
        tail = lax.slice_in_dim(cells, cells.shape[dim] - width, cells.shape[dim], axis=dim)
        cells = jnp.concatenate(
            [
                lax.ppermute(tail, axis, [(i, (i + 1) % count) for i in range(count)]),
                cells,
                lax.ppermute(head, axis, [((i + 1) % count, i) for i in range(count)]),
            ],
            axis=dim,
        )
    return cells


def passed_along(block, axis, distance):
    devices = range(lax.axis_size(axis))
    route = [((i - distance) % len(devices), i) for i in devices]
    return lax.ppermute(block, axis, route)


def dft_table(size):
    rows = lax.broadcasted_iota(jnp.int32, (size, size), 0)
    cols = lax.broadcasted_iota(jnp.int32, (size, size), 1)
    angle = (rows * cols % size).astype(jnp.float32) * (2.0 * math.pi / size)
    return (jnp.cos(angle), jnp.sin(angle))


def toeplitz(kernels):
    width = kernels.shape[-1]
    tail = jnp.zeros(kernels.shape[:-1] + (width + 1,), kernels.dtype)
    padded = jnp.concatenate([kernels, tail], -1)
    tiled = jnp.tile(padded, (1, 1, width))[..., : 2 * width * width]
    return tiled.reshape(kernels.shape[:-1] + (width, 2 * width))


def take_blocks(joined, start):
    return lax.dynamic_slice_in_dim(joined, start, joined.shape[0] // 2, 0)


def slide(joined, starts):
    return jax.vmap(jax.vmap(take_blocks))(joined, starts)


def general(samples, kernels, offsets, weight_index, level_weights):
    segs, comps, rows_one, cols_two = samples.shape
    ranks = lax.axis_size("freq")
    here = lax.axis_index("freq")
    size_one = rows_one * ranks
    length = size_one * cols_two
    highest = lax.Precision.HIGHEST
    cos_two, sin_two = dft_table(cols_two)
    stacked = samples.reshape(segs * comps * rows_one, cols_two)
    with_cos = jnp.dot(stacked, cos_two, precision=highest).reshape(samples.shape)
    with_sin = jnp.dot(stacked, sin_two, precision=highest).reshape(samples.shape)
    first_real = with_cos[:, 0] + with_sin[:, 1]
    first_imag = with_cos[:, 1] - with_sin[:, 0]
    row_global = here * rows_one + lax.broadcasted_iota(jnp.int32, (rows_one, cols_two), 0)
    col_global = lax.broadcasted_iota(jnp.int32, (rows_one, cols_two), 1)
    twist = (row_global * col_global % length).astype(jnp.float32) * (2.0 * math.pi / length)
    twist_cos = jnp.cos(twist)
    twist_sin = jnp.sin(twist)
    turned = jnp.stack(
        [
            first_real * twist_cos + first_imag * twist_sin,
            first_imag * twist_cos - first_real * twist_sin,
        ],
        1,
    )
    columns = lax.all_to_all(
        turned.astype(jnp.bfloat16), "freq", split_axis=3, concat_axis=3, tiled=True
    ).astype(turned.dtype)
    width_two = cols_two // ranks
    ordered = columns.reshape(segs, comps, rows_one, ranks, width_two)
    cos_one, sin_one = dft_table(size_one)
    cos_one = cos_one.reshape(ranks, rows_one, size_one)
    sin_one = sin_one.reshape(ranks, rows_one, size_one)
    second_cos = jnp.einsum("scirl,rik->sclk", ordered, cos_one, precision=highest)
    second_sin = jnp.einsum("scirl,rik->sclk", ordered, sin_one, precision=highest)
    second = jnp.stack(
        [second_cos[:, 0] + second_sin[:, 1], second_cos[:, 1] - second_sin[:, 0]], 1
    )
    arrived = lax.all_to_all(
        second.astype(jnp.bfloat16), "freq", split_axis=3, concat_axis=3, tiled=True
    ).astype(second.dtype)
    width_one = size_one // ranks
    spectrum = arrived.reshape(segs, comps, width_two, ranks, width_one)
    spectrum = jnp.transpose(spectrum, (0, 1, 4, 3, 2)).reshape(segs, comps, width_one * cols_two)
    spectrum = (spectrum * (1.0 / math.sqrt(length))).astype(jnp.bfloat16)
    half = BLOCK // 2
    edged = extended(spectrum, (("freq", 2),), half)
    bins_here = spectrum.shape[2]
    count = bins_here // BLOCK
    lower = edged[..., :bins_here].reshape(segs, comps, count, BLOCK)
    upper = edged[..., BLOCK:].reshape(segs, comps, count, BLOCK)
    window = jnp.concatenate([lower, upper], -1)
    bands = toeplitz(kernels)
    real_band = bands[0]
    imag_band = bands[1]
    table = jnp.stack(
        [jnp.stack([real_band, imag_band], 0), jnp.stack([-imag_band, real_band], 0)], 0
    )
    filtered = jnp.einsum("scbm,cokim->skboi", window, table, preferred_element_type=jnp.float32)
    power = (filtered[:, :, :, 0] ** 2 + filtered[:, :, :, 1] ** 2).astype(jnp.bfloat16)
    quotient = jnp.floor_divide(offsets, count)
    remainder = offsets - quotient * count
    following = passed_along(power, "freq", -1)
    inner = slide(jnp.concatenate([power, following], 2), remainder)
    plane_count = segs * KERNELS
    flat = inner.reshape(plane_count, count * BLOCK)
    plane_quot = quotient.reshape(plane_count)
    distances = lax.broadcasted_iota(jnp.int32, (2 * REACH + 1, plane_count), 0) - REACH
    member = (plane_quot[None, :] == distances).astype(jnp.int32)
    earlier = lax.broadcasted_iota(jnp.int32, (plane_count, plane_count), 0)
    later = lax.broadcasted_iota(jnp.int32, (plane_count, plane_count), 1)
    place = jnp.sum(jnp.where(earlier <= later, member[:, :, None], 0), 1) - 1
    slot_ids = lax.broadcasted_iota(jnp.int32, (2 * REACH + 1, ROUTE_CAP, plane_count), 1)
    select = ((member[:, None, :] == 1) & (place[:, None, :] == slot_ids)).astype(jnp.bfloat16)
    packed = jnp.einsum("dcp,pl->dcl", select, flat, preferred_element_type=jnp.float32).astype(
        jnp.bfloat16
    )
    received = []
    for step_index in range(2 * REACH + 1):
        received.append(passed_along(packed[step_index], "freq", -(step_index - REACH)))
    gathered = jnp.stack(received, 0)
    placed = jnp.einsum("dcp,dcl->pl", select, gathered, preferred_element_type=jnp.float32)
    shifted = placed.astype(jnp.bfloat16).reshape(segs, KERNELS, count, BLOCK)
    levels = lax.broadcasted_iota(jnp.int32, (segs, level_weights.shape[0]), 1)
    weights = jnp.sum(jnp.where(weight_index[:, None] == levels, level_weights[None, :], 0.0), 1)
    scale = 1.0 / (segs * lax.axis_size("seg"))
    partial_sum = jnp.sum((weights * scale)[:, None, None, None] * shifted.astype(jnp.float32), 0)
    owned = lax.psum_scatter(
        partial_sum.astype(jnp.bfloat16), "seg", scatter_dimension=0, tiled=True
    ).astype(jnp.float32)
    return owned.reshape(owned.shape[0], count * BLOCK)


VMEM = pl.BlockSpec(memory_space=pltpu.VMEM)
SMEM = pl.BlockSpec(memory_space=pltpu.SMEM)
PAD = 16
RADIX = 4
LEAD = 3
BF16 = jnp.bfloat16
F32 = jnp.float32


def unit(turns, scale=1.0):
    angle = 2.0 * np.pi * turns
    return (np.cos(angle) * scale).astype(np.float32), (np.sin(angle) * scale).astype(np.float32)


def first_waves(size):
    turns = np.arange(size)[:, None] * (np.arange(size) - BLOCK // 2)[None, :] % size / size
    both = np.stack([x.reshape(size, size // BLOCK, BLOCK) for x in unit(turns)], 2)
    return np.transpose(both, (1, 0, 2, 3)).reshape(size // BLOCK, size, 2 * BLOCK).astype(BF16)


def second_waves(size):
    quarter = size // RADIX
    places = np.arange(quarter)[None, None, :] * RADIX + np.arange(RADIX)[:, None, None]
    turns = np.arange(quarter)[None, :, None] * places % size / size
    return np.concatenate(unit(turns), 1).astype(BF16)


def fill_bands(taps_ref, band_ref):
    wide = 2 * BLOCK
    for t in range(taps_ref.shape[1]):
        both = []
        for c in range(2):
            row = taps_ref[c, t : t + 1, :].astype(F32)
            row = jnp.concatenate([row, jnp.zeros_like(row)], 1)
            row = jnp.broadcast_to(row, (BLOCK, wide))
            both.append(pltpu.roll(row, 0, 1, stride=1, stride_axis=0).T)
        re, im = both
        band_ref[t, :wide, :BLOCK] = re.astype(BF16)
        band_ref[t, :wide, BLOCK:] = im.astype(BF16)
        band_ref[t, wide:, :BLOCK] = (-im).astype(BF16)
        band_ref[t, wide:, BLOCK:] = re.astype(BF16)


def remote(src, dst, sems, at, axis, device):
    return pltpu.make_async_remote_copy(
        src_ref=src,
        dst_ref=dst,
        send_sem=sems[0].at[at],
        recv_sem=sems[1].at[at],
        device_id={axis: device},
        device_id_type=pl.DeviceIdType.MESH,
    )


def first_step(segs, rows, table_ref, xb_ref, near_ref, far_ref, mixed_ref, me, j):
    lanes = pl.ds(pl.multiple_of(j * BLOCK, BLOCK), BLOCK)
    got = jnp.dot(xb_ref[...], table_ref[j], preferred_element_type=F32)
    a = far_ref[me, 0:1, lanes]
    b = far_ref[me, 1:2, lanes]
    near_cos = near_ref[j, :rows]
    near_sin = near_ref[j, rows:]
    wc = a * near_cos - b * near_sin
    ws = b * near_cos + a * near_sin
    for s in range(segs):
        top = got[2 * s * rows : (2 * s + 1) * rows]
        low = got[(2 * s + 1) * rows : (2 * s + 2) * rows]
        re = top[:, :BLOCK] + low[:, BLOCK:]
        im = low[:, :BLOCK] - top[:, BLOCK:]
        mixed_ref[2 * s] = re * wc + im * ws
        mixed_ref[2 * s + 1] = im * wc - re * ws


def second_step(segs, wave_ref, turned_ref, w_ref, j):
    wide = 2 * BLOCK
    quarter = wave_ref.shape[1] // 2
    total = quarter * RADIX
    tall = w_ref.shape[3] - total
    for s in range(segs):
        terms = []
        for c in range(RADIX):
            y = jnp.dot(
                wave_ref[c], turned_ref[j, c, :, s * wide : (s + 1) * wide], preferred_element_type=F32
            )
            re = y[:quarter, :BLOCK] + y[quarter:, BLOCK:]
            im = y[:quarter, BLOCK:] - y[quarter:, :BLOCK]
            terms.append((re, im))
        (r0, i0), (r1, i1), (r2, i2), (r3, i3) = terms
        re = (r0 + r2) + (r1 + r3), (r0 - r2) + (i1 - i3), (r0 + r2) - (r1 + r3), (r0 - r2) - (i1 - i3)
        im = (i0 + i2) + (i1 + i3), (i0 - i2) - (r1 - r3), (i0 + i2) - (i1 + i3), (i0 - i2) + (r1 - r3)
        for m in range(RADIX):
            here = slice(m * quarter, (m + 1) * quarter)
            w_ref[s, 0, j, here, :] = re[m].astype(BF16)
            w_ref[s, 1, j, here, :] = im[m].astype(BF16)
        for c in range(2):
            w_ref[s, c, j, total:, :] = w_ref[s, c, j, :tall, :]


def wrap_column(w_ref, total):
    segs, comps, columns, high, _ = w_ref.shape
    for s in range(segs):
        for c in range(comps):
            x = w_ref[s, c, 0, :total, :].astype(F32)
            w_ref[s, c, columns - 1, :total, :] = jnp.concatenate([x[1:], x[:1]], 0).astype(BF16)
            w_ref[s, c, columns - 1, total:, :] = w_ref[s, c, columns - 1, : high - total, :]


def source_of(off_ref, s, t, total, ranks):
    blocks = total * ranks
    base = lax.rem(lax.axis_index("freq") * total + off_ref[s, t] + blocks, blocks)
    return base // ranks, lax.rem(base, ranks)


def filter_some(w_ref, band_ref, p_ref, power_ref, off_ref, weights, first, columns, rows, ranks, low, high):
    segs = len(weights)
    total = rows * ranks
    tall = rows + PAD
    count = band_ref.shape[0]

    @pl.loop(low, high, unroll=min(4, high - low))
    def _(i):
        t = lax.rem(first + i, count)
        parts = []
        shifts = []
        for s in range(segs):
            gk, gj = source_of(off_ref, s, t, total, ranks)
            for j in columns:
                row = lax.rem(gk + (gj - j + ranks - 1) // ranks, total)
                start = row // PAD * PAD
                shifts.append(row - start)
                take = pl.ds(start, tall)
                pieces = [w_ref[s, c, j + e, take, :] for c in range(2) for e in range(2)]
                parts.append(jnp.concatenate(pieces, 1))
        got = jnp.dot(jnp.concatenate(parts, 0), band_ref[t], preferred_element_type=F32)
        re = got[:, :BLOCK]
        im = got[:, BLOCK:]
        p_ref[...] = re * re + im * im
        for s in range(segs):
            for n, j in enumerate(columns):
                at = s * len(columns) + n
                x = p_ref[pl.ds(at * tall + shifts[at], rows), :]
                power_ref[i, s, j] = (weights[s] * x).astype(BF16)


def gather_kernel(
    x_hbm, first_hbm, near_hbm, far_hbm, wave_hbm, taps_hbm, off_hbm, wi_hbm, lw_hbm,
    power_ref, got_ref,
    x_ref, table_ref, near_ref, far_ref, wave_ref, taps_ref, off_ref, wi_ref, lw_ref,
    xb_ref, mixed_ref, turned_ref, w_ref, band_ref, p_ref, send_ref,
    in_sem,
    ring_send, ring_recv, core_send, core_recv,
):
    segs, comps, rows, cols = x_ref.shape
    ranks = lax.axis_size("freq")
    total = rows * ranks
    hops = ranks // 2
    part = rows // RADIX
    me = lax.axis_index("freq")
    core = lax.axis_index("seg")
    half = got_ref.shape[0]

    rest = slice(1, ranks)
    pairs = [
        (x_hbm.at[0], x_ref.at[0]), (x_hbm.at[1], x_ref.at[1]), (first_hbm.at[0], table_ref.at[0]),
        (near_hbm.at[0], near_ref.at[0]), (far_hbm, far_ref),
        (first_hbm.at[rest], table_ref.at[rest]), (near_hbm.at[rest], near_ref.at[rest]),
        (off_hbm, off_ref), (wi_hbm, wi_ref), (lw_hbm, lw_ref), (taps_hbm, taps_ref), (wave_hbm, wave_ref),
    ]
    fetches = [pltpu.make_async_copy(src, dst, in_sem.at[n]) for n, (src, dst) in enumerate(pairs)]
    for fetch in fetches[:7]:
        fetch.start()

    odd = me % 2
    place = (1 - odd) * (me // 2) + odd * (ranks - 1 - me // 2)

    def at_place(p):
        p = (p + ranks) % ranks
        far = p // (ranks // 2)
        return (1 - far) * (2 * p) + far * (2 * (ranks - 1 - p) + 1)

    barrier = pltpu.get_barrier_semaphore()
    for peer in (at_place(place + 1), at_place(place - 1)):
        pl.semaphore_signal(barrier, inc=1, device_id={"freq": peer}, device_id_type=pl.DeviceIdType.MESH)
    pl.semaphore_signal(barrier, inc=1, device_id={"seg": 1 - core}, device_id_type=pl.DeviceIdType.MESH)

    def moved(j, k, way, origin):
        owner = at_place(place - origin) if way == 0 else at_place(place + origin)
        target = at_place(place + 1) if way == 0 else at_place(place - 1)
        classes = pl.ds(0, RADIX) if k < hops - 1 else pl.ds(way * (RADIX // 2), RADIX // 2)
        block = turned_ref.at[j, classes, pl.ds(pl.multiple_of(owner * part, part), part), :]
        return remote(block, block, (ring_send, ring_recv), (way, j, k), "freq", target)

    def send(j, k):
        for way in range(2):
            moved(j, k, way, k).start()

    def landed(j, k):
        for way in range(2):
            moved(j, k, way, k + 1).wait_recv()

    own_rows = pl.ds(pl.multiple_of(me * part, part), part)
    for s in range(segs):
        fetches[s].wait()
        for c in range(comps):
            at = (s * comps + c) * rows
            xb_ref[at : at + rows, :] = x_ref[s, c].astype(BF16)
    for fetch in fetches[2:5]:
        fetch.wait()
    for fetch in fetches[7:]:
        fetch.start()

    @pl.loop(0, ranks)
    def _(j):
        @pl.when(j == 1)
        def _():
            for fetch in fetches[5:7]:
                fetch.wait()

        first_step(segs, rows, table_ref, xb_ref, near_ref, far_ref, mixed_ref, me, j)
        for n in range(RADIX):
            for i in range(segs * comps):
                lanes = slice(i * BLOCK, (i + 1) * BLOCK)
                turned_ref[j, n, own_rows, lanes] = mixed_ref[i, pl.ds(n, part, stride=RADIX), :].astype(BF16)

        @pl.when(j == 0)
        def _():
            pl.semaphore_wait(barrier, 3)

        @pl.when(j < LEAD)
        def _():
            send(j, 0)

    for fetch in fetches[7:]:
        fetch.wait()
    weights = [lw_ref[wi_ref[s]] * (1.0 / (2 * segs)) for s in range(segs)]
    sift = functools.partial(filter_some, w_ref, band_ref, p_ref, power_ref, off_ref, weights, core * half)

    @pl.loop(0, ranks + hops - 1)
    def _(q):
        @pl.when(q < ranks)
        def _():
            landed(q, 0)
            send(q, 1)

        @pl.when(q < ranks - LEAD)
        def _():
            send(q + LEAD, 0)

        @pl.when(q == 0)
        def _():
            fill_bands(taps_ref, band_ref)

        for k in range(1, hops - 1):

            @pl.when((q >= k) & (q < ranks + k))
            def _():
                landed(q - k, k)
                send(q - k, k + 1)

        for pair in range(ranks // 2 - 1):

            @pl.when(q == 2 * pair + hops + 2)
            def _():
                sift((2 * pair, 2 * pair + 1), rows, ranks, 0, 2 * half)

        @pl.when(q >= hops - 1)
        def _():
            landed(q - hops + 1, hops - 1)
            second_step(segs, wave_ref, turned_ref, w_ref, q - hops + 1)

        @pl.when(q == hops - 1)
        def _():
            wrap_column(w_ref, total)

    def swap(i):
        return remote(send_ref.at[i], got_ref.at[i], (core_send, core_recv), (i,), "seg", 1 - core)

    for part_of in range(2):
        low = half + part_of * (half // 2)
        sift((ranks - 2, ranks - 1), rows, ranks, low, low + half // 2)

        @pl.loop(low - half, low - half + half // 2)
        def _(i):
            t = (1 - core) * half + i
            turns = [source_of(off_ref, s, t, total, ranks)[1] for s in range(segs)]
            for jj in range(ranks):
                x = sum(power_ref[half + i, s, lax.rem(turns[s] + jj, ranks)].astype(F32) for s in range(segs))
                send_ref[i, jj] = x.astype(BF16)
            swap(i).start()

    sift((ranks - 2, ranks - 1), rows, ranks, 0, half)

    @pl.loop(0, half)
    def _(i):
        swap(i).wait()

    @pl.loop(0, ranks)
    def _(j):
        for k in range(hops):
            for way in range(2):
                moved(j, k, way, k).wait_send()


def combine_kernel(off_ref, power_ref, got_ref, out_ref, sum_ref, sems):
    half, ranks, rows, _ = got_ref.shape
    segs = power_ref.shape[1]
    core = lax.axis_index("seg")
    copies = []
    for i in range(half):
        turns = [source_of(off_ref, s, core * half + i, rows * ranks, ranks)[1] for s in range(segs)]
        for jj in range(ranks):
            x = got_ref[i, jj].astype(F32)
            for s in range(segs):
                x = x + power_ref[i, s, lax.rem(turns[s] + jj, ranks)].astype(F32)
            sum_ref[i, jj] = x
            copy = pltpu.make_async_copy(sum_ref.at[i, jj], out_ref.at[:, jj, i, :], sems.at[i, jj])
            copy.start()
            copies.append(copy)
    for copy in copies:
        copy.wait()


def body(samples, kernels, offsets, weight_index, level_weights):
    segs, comps, rows, cols = samples.shape
    ranks = lax.axis_size("freq")
    size_one = rows * ranks
    if cols != ranks * BLOCK or rows != BLOCK or size_one != cols or segs != 2 or lax.axis_size("seg") != 2:
        return general(samples, kernels, offsets, weight_index, level_weights)
    length = size_one * cols
    bins = np.arange(cols) - BLOCK // 2
    near = unit(np.arange(rows)[:, None] * bins[None, :] % length / length, 1.0 / math.sqrt(length))
    far = unit(np.arange(ranks)[:, None] * rows * bins[None, :] % length / length)
    count = kernels.shape[1]
    half = count // 2
    tall = rows + PAD
    hops = ranks // 2
    copies = pltpu.SemaphoreType.DMA
    near = np.transpose(np.concatenate(near).reshape(2 * rows, ranks, BLOCK), (1, 0, 2))
    constants = [first_waves(cols), near, np.stack(far, 1), second_waves(size_one)]
    operands = [samples, *(jnp.asarray(x) for x in constants), kernels, offsets, weight_index, level_weights]
    shapes = [pltpu.VMEM(x.shape, x.dtype) for x in operands[:6]] + [pltpu.SMEM(x.shape, x.dtype) for x in operands[6:]]
    power, got = pl.pallas_call(
        gather_kernel,
        out_shape=(
            jax.ShapeDtypeStruct((count, segs, ranks, rows, BLOCK), BF16),
            jax.ShapeDtypeStruct((half, ranks, rows, BLOCK), BF16),
        ),
        in_specs=[pl.BlockSpec(memory_space=pltpu.HBM)] * len(operands),
        out_specs=(VMEM, VMEM),
        scratch_shapes=shapes
        + [
            pltpu.VMEM((segs * comps * rows, cols), BF16),
            pltpu.VMEM((segs * comps, rows, BLOCK), F32),
            pltpu.VMEM((ranks, RADIX, size_one // RADIX, segs * comps * BLOCK), BF16),
            pltpu.VMEM((segs, comps, ranks + 1, size_one + tall, BLOCK), BF16),
            pltpu.VMEM((count, 4 * BLOCK, 2 * BLOCK), BF16),
            pltpu.VMEM((2 * segs * tall, BLOCK), F32),
            pltpu.VMEM((half, ranks, rows, BLOCK), BF16),
        ]
        + [copies((12,))]
        + [copies((2, ranks, hops))] * 2
        + [copies((half,))] * 2,
        compiler_params=pltpu.CompilerParams(vmem_limit_bytes=48 << 20, collective_id=0, has_side_effects=True),
    )(*(pltpu.with_memory_space_constraint(x, pltpu.HBM) for x in operands))
    out = pl.pallas_call(
        combine_kernel,
        out_shape=jax.ShapeDtypeStruct((rows, ranks, half, BLOCK), F32),
        in_specs=[SMEM, VMEM, VMEM],
        out_specs=pl.BlockSpec(memory_space=pltpu.HBM),
        scratch_shapes=[pltpu.VMEM((half, ranks, rows, BLOCK), F32), copies((half, ranks))],
        compiler_params=pltpu.CompilerParams(vmem_limit_bytes=24 << 20),
    )(offsets, power, got)
    return jnp.transpose(out.reshape(rows * ranks, half, BLOCK), (1, 0, 2)).reshape(half, rows * cols)


def solution(mesh):
    in_specs = (
        P(("parts", "seg"), None, "freq", None),
        P(),
        P(("parts", "seg"), None),
        P(("parts", "seg")),
        P(),
    )
    out_specs = P(("parts", "seg"), "freq")
    return jax.shard_map(body, mesh=mesh, in_specs=in_specs, out_specs=out_specs, check_vma=False)
```

```python
import math

import functools

import jax
import jax.numpy as jnp
import numpy as np
from jax import lax
from jax.experimental import pallas as pl
from jax.experimental.pallas import tpu as pltpu
from jax.sharding import PartitionSpec as P

BLOCK = 128
KERNELS = 8
REACH = 4
ROUTE_CAP = 4


def extended(cells, sides, width):
    for axis, dim in sides:
        count = lax.axis_size(axis)
        head = lax.slice_in_dim(cells, 0, width, axis=dim)
        tail = lax.slice_in_dim(cells, cells.shape[dim] - width, cells.shape[dim], axis=dim)
        cells = jnp.concatenate(
            [
                lax.ppermute(tail, axis, [(i, (i + 1) % count) for i in range(count)]),
                cells,
                lax.ppermute(head, axis, [((i + 1) % count, i) for i in range(count)]),
            ],
            axis=dim,
        )
    return cells


def passed_along(block, axis, distance):
    devices = range(lax.axis_size(axis))
    route = [((i - distance) % len(devices), i) for i in devices]
    return lax.ppermute(block, axis, route)


def dft_table(size):
    rows = lax.broadcasted_iota(jnp.int32, (size, size), 0)
    cols = lax.broadcasted_iota(jnp.int32, (size, size), 1)
    angle = (rows * cols % size).astype(jnp.float32) * (2.0 * math.pi / size)
    return (jnp.cos(angle), jnp.sin(angle))


def toeplitz(kernels):
    width = kernels.shape[-1]
    tail = jnp.zeros(kernels.shape[:-1] + (width + 1,), kernels.dtype)
    padded = jnp.concatenate([kernels, tail], -1)
    tiled = jnp.tile(padded, (1, 1, width))[..., : 2 * width * width]
    return tiled.reshape(kernels.shape[:-1] + (width, 2 * width))


def take_blocks(joined, start):
    return lax.dynamic_slice_in_dim(joined, start, joined.shape[0] // 2, 0)


def slide(joined, starts):
    return jax.vmap(jax.vmap(take_blocks))(joined, starts)


def general(samples, kernels, offsets, weight_index, level_weights):
    segs, comps, rows_one, cols_two = samples.shape
    ranks = lax.axis_size("freq")
    here = lax.axis_index("freq")
    size_one = rows_one * ranks
    length = size_one * cols_two
    highest = lax.Precision.HIGHEST
    cos_two, sin_two = dft_table(cols_two)
    stacked = samples.reshape(segs * comps * rows_one, cols_two)
    with_cos = jnp.dot(stacked, cos_two, precision=highest).reshape(samples.shape)
    with_sin = jnp.dot(stacked, sin_two, precision=highest).reshape(samples.shape)
    first_real = with_cos[:, 0] + with_sin[:, 1]
    first_imag = with_cos[:, 1] - with_sin[:, 0]
    row_global = here * rows_one + lax.broadcasted_iota(jnp.int32, (rows_one, cols_two), 0)
    col_global = lax.broadcasted_iota(jnp.int32, (rows_one, cols_two), 1)
    twist = (row_global * col_global % length).astype(jnp.float32) * (2.0 * math.pi / length)
    twist_cos = jnp.cos(twist)
    twist_sin = jnp.sin(twist)
    turned = jnp.stack(
        [
            first_real * twist_cos + first_imag * twist_sin,
            first_imag * twist_cos - first_real * twist_sin,
        ],
        1,
    )
    columns = lax.all_to_all(
        turned.astype(jnp.bfloat16), "freq", split_axis=3, concat_axis=3, tiled=True
    ).astype(turned.dtype)
    width_two = cols_two // ranks
    ordered = columns.reshape(segs, comps, rows_one, ranks, width_two)
    cos_one, sin_one = dft_table(size_one)
    cos_one = cos_one.reshape(ranks, rows_one, size_one)
    sin_one = sin_one.reshape(ranks, rows_one, size_one)
    second_cos = jnp.einsum("scirl,rik->sclk", ordered, cos_one, precision=highest)
    second_sin = jnp.einsum("scirl,rik->sclk", ordered, sin_one, precision=highest)
    second = jnp.stack(
        [second_cos[:, 0] + second_sin[:, 1], second_cos[:, 1] - second_sin[:, 0]], 1
    )
    arrived = lax.all_to_all(
        second.astype(jnp.bfloat16), "freq", split_axis=3, concat_axis=3, tiled=True
    ).astype(second.dtype)
    width_one = size_one // ranks
    spectrum = arrived.reshape(segs, comps, width_two, ranks, width_one)
    spectrum = jnp.transpose(spectrum, (0, 1, 4, 3, 2)).reshape(segs, comps, width_one * cols_two)
    spectrum = (spectrum * (1.0 / math.sqrt(length))).astype(jnp.bfloat16)
    half = BLOCK // 2
    edged = extended(spectrum, (("freq", 2),), half)
    bins_here = spectrum.shape[2]
    count = bins_here // BLOCK
    lower = edged[..., :bins_here].reshape(segs, comps, count, BLOCK)
    upper = edged[..., BLOCK:].reshape(segs, comps, count, BLOCK)
    window = jnp.concatenate([lower, upper], -1)
    bands = toeplitz(kernels)
    real_band = bands[0]
    imag_band = bands[1]
    table = jnp.stack(
        [jnp.stack([real_band, imag_band], 0), jnp.stack([-imag_band, real_band], 0)], 0
    )
    filtered = jnp.einsum("scbm,cokim->skboi", window, table, preferred_element_type=jnp.float32)
    power = (filtered[:, :, :, 0] ** 2 + filtered[:, :, :, 1] ** 2).astype(jnp.bfloat16)
    quotient = jnp.floor_divide(offsets, count)
    remainder = offsets - quotient * count
    following = passed_along(power, "freq", -1)
    inner = slide(jnp.concatenate([power, following], 2), remainder)
    plane_count = segs * KERNELS
    flat = inner.reshape(plane_count, count * BLOCK)
    plane_quot = quotient.reshape(plane_count)
    distances = lax.broadcasted_iota(jnp.int32, (2 * REACH + 1, plane_count), 0) - REACH
    member = (plane_quot[None, :] == distances).astype(jnp.int32)
    earlier = lax.broadcasted_iota(jnp.int32, (plane_count, plane_count), 0)
    later = lax.broadcasted_iota(jnp.int32, (plane_count, plane_count), 1)
    place = jnp.sum(jnp.where(earlier <= later, member[:, :, None], 0), 1) - 1
    slot_ids = lax.broadcasted_iota(jnp.int32, (2 * REACH + 1, ROUTE_CAP, plane_count), 1)
    select = ((member[:, None, :] == 1) & (place[:, None, :] == slot_ids)).astype(jnp.bfloat16)
    packed = jnp.einsum("dcp,pl->dcl", select, flat, preferred_element_type=jnp.float32).astype(
        jnp.bfloat16
    )
    received = []
    for step_index in range(2 * REACH + 1):
        received.append(passed_along(packed[step_index], "freq", -(step_index - REACH)))
    gathered = jnp.stack(received, 0)
    placed = jnp.einsum("dcp,dcl->pl", select, gathered, preferred_element_type=jnp.float32)
    shifted = placed.astype(jnp.bfloat16).reshape(segs, KERNELS, count, BLOCK)
    levels = lax.broadcasted_iota(jnp.int32, (segs, level_weights.shape[0]), 1)
    weights = jnp.sum(jnp.where(weight_index[:, None] == levels, level_weights[None, :], 0.0), 1)
    scale = 1.0 / (segs * lax.axis_size("seg"))
    partial_sum = jnp.sum((weights * scale)[:, None, None, None] * shifted.astype(jnp.float32), 0)
    owned = lax.psum_scatter(
        partial_sum.astype(jnp.bfloat16), "seg", scatter_dimension=0, tiled=True
    ).astype(jnp.float32)
    return owned.reshape(owned.shape[0], count * BLOCK)


VMEM = pl.BlockSpec(memory_space=pltpu.VMEM)
SMEM = pl.BlockSpec(memory_space=pltpu.SMEM)
PAD = 16
RADIX = 4
LEAD = 3
BF16 = jnp.bfloat16
F32 = jnp.float32


def unit(turns, scale=1.0):
    angle = 2.0 * np.pi * turns
    return (np.cos(angle) * scale).astype(np.float32), (np.sin(angle) * scale).astype(np.float32)


def first_waves(size):
    turns = np.arange(size)[:, None] * (np.arange(size) - BLOCK // 2)[None, :] % size / size
    both = np.stack([x.reshape(size, size // BLOCK, BLOCK) for x in unit(turns)], 2)
    return np.transpose(both, (1, 0, 2, 3)).reshape(size // BLOCK, size, 2 * BLOCK).astype(BF16)


def second_waves(size):
    quarter = size // RADIX
    places = np.arange(quarter)[None, None, :] * RADIX + np.arange(RADIX)[:, None, None]
    turns = np.arange(quarter)[None, :, None] * places % size / size
    return np.concatenate(unit(turns), 1).astype(BF16)


def fill_bands(taps_ref, band_ref):
    wide = 2 * BLOCK
    for t in range(taps_ref.shape[1]):
        both = []
        for c in range(2):
            row = taps_ref[c, t : t + 1, :].astype(F32)
            row = jnp.concatenate([row, jnp.zeros_like(row)], 1)
            row = jnp.broadcast_to(row, (BLOCK, wide))
            both.append(pltpu.roll(row, 0, 1, stride=1, stride_axis=0).T)
        re, im = both
        band_ref[t, :wide, :BLOCK] = re.astype(BF16)
        band_ref[t, :wide, BLOCK:] = im.astype(BF16)
        band_ref[t, wide:, :BLOCK] = (-im).astype(BF16)
        band_ref[t, wide:, BLOCK:] = re.astype(BF16)


def remote(src, dst, sems, at, axis, device):
    return pltpu.make_async_remote_copy(
        src_ref=src,
        dst_ref=dst,
        send_sem=sems[0].at[at],
        recv_sem=sems[1].at[at],
        device_id={axis: device},
        device_id_type=pl.DeviceIdType.MESH,
    )


def first_step(segs, rows, table_ref, xb_ref, near_ref, far_ref, mixed_ref, me, j):
    lanes = pl.ds(pl.multiple_of(j * BLOCK, BLOCK), BLOCK)
    got = jnp.dot(xb_ref[...], table_ref[j], preferred_element_type=F32)
    a = far_ref[me, 0:1, lanes]
    b = far_ref[me, 1:2, lanes]
    near_cos = near_ref[j, :rows]
    near_sin = near_ref[j, rows:]
    wc = a * near_cos - b * near_sin
    ws = b * near_cos + a * near_sin
    for s in range(segs):
        top = got[2 * s * rows : (2 * s + 1) * rows]
        low = got[(2 * s + 1) * rows : (2 * s + 2) * rows]
        re = top[:, :BLOCK] + low[:, BLOCK:]
        im = low[:, :BLOCK] - top[:, BLOCK:]
        mixed_ref[2 * s] = re * wc + im * ws
        mixed_ref[2 * s + 1] = im * wc - re * ws


def second_step(segs, wave_ref, turned_ref, w_ref, j):
    wide = 2 * BLOCK
    quarter = wave_ref.shape[1] // 2
    total = quarter * RADIX
    tall = w_ref.shape[3] - total
    for s in range(segs):
        terms = []
        for c in range(RADIX):
            y = jnp.dot(
                wave_ref[c], turned_ref[j, c, :, s * wide : (s + 1) * wide], preferred_element_type=F32
            )
            re = y[:quarter, :BLOCK] + y[quarter:, BLOCK:]
            im = y[:quarter, BLOCK:] - y[quarter:, :BLOCK]
            terms.append((re, im))
        (r0, i0), (r1, i1), (r2, i2), (r3, i3) = terms
        re = (r0 + r2) + (r1 + r3), (r0 - r2) + (i1 - i3), (r0 + r2) - (r1 + r3), (r0 - r2) - (i1 - i3)
        im = (i0 + i2) + (i1 + i3), (i0 - i2) - (r1 - r3), (i0 + i2) - (i1 + i3), (i0 - i2) + (r1 - r3)
        for m in range(RADIX):
            here = slice(m * quarter, (m + 1) * quarter)
            w_ref[s, 0, j, here, :] = re[m].astype(BF16)
            w_ref[s, 1, j, here, :] = im[m].astype(BF16)
        for c in range(2):
            w_ref[s, c, j, total:, :] = w_ref[s, c, j, :tall, :]


def wrap_column(w_ref, total):
    segs, comps, columns, high, _ = w_ref.shape
    for s in range(segs):
        for c in range(comps):
            x = w_ref[s, c, 0, :total, :].astype(F32)
            w_ref[s, c, columns - 1, :total, :] = jnp.concatenate([x[1:], x[:1]], 0).astype(BF16)
            w_ref[s, c, columns - 1, total:, :] = w_ref[s, c, columns - 1, : high - total, :]


def source_of(off_ref, s, t, total, ranks):
    blocks = total * ranks
    base = lax.rem(lax.axis_index("freq") * total + off_ref[s, t] + blocks, blocks)
    return base // ranks, lax.rem(base, ranks)


def filter_some(w_ref, band_ref, p_ref, power_ref, off_ref, weights, first, columns, rows, ranks, low, high):
    segs = len(weights)
    total = rows * ranks
    tall = rows + PAD
    count = band_ref.shape[0]

    @pl.loop(low, high, unroll=min(4, high - low))
    def _(i):
        t = lax.rem(first + i, count)
        parts = []
        shifts = []
        for s in range(segs):
            gk, gj = source_of(off_ref, s, t, total, ranks)
            for j in columns:
                row = lax.rem(gk + (gj - j + ranks - 1) // ranks, total)
                start = row // PAD * PAD
                shifts.append(row - start)
                take = pl.ds(start, tall)
                pieces = [w_ref[s, c, j + e, take, :] for c in range(2) for e in range(2)]
                parts.append(jnp.concatenate(pieces, 1))
        got = jnp.dot(jnp.concatenate(parts, 0), band_ref[t], preferred_element_type=F32)
        re = got[:, :BLOCK]
        im = got[:, BLOCK:]
        p_ref[...] = re * re + im * im
        for s in range(segs):
            for n, j in enumerate(columns):
                at = s * len(columns) + n
                x = p_ref[pl.ds(at * tall + shifts[at], rows), :]
                power_ref[i, s, j] = (weights[s] * x).astype(BF16)


def gather_kernel(
    x_hbm, first_hbm, near_hbm, far_hbm, wave_hbm, taps_hbm, off_hbm, wi_hbm, lw_hbm,
    power_ref, got_ref,
    x_ref, table_ref, near_ref, far_ref, wave_ref, taps_ref, off_ref, wi_ref, lw_ref,
    xb_ref, mixed_ref, turned_ref, w_ref, band_ref, p_ref, send_ref,
    in_sem,
    ring_send, ring_recv, core_send, core_recv,
):
    segs, comps, rows, cols = x_ref.shape
    ranks = lax.axis_size("freq")
    total = rows * ranks
    hops = ranks // 2
    part = rows // RADIX
    me = lax.axis_index("freq")
    core = lax.axis_index("seg")
    half = got_ref.shape[0]

    rest = slice(1, ranks)
    pairs = [
        (x_hbm.at[0], x_ref.at[0]), (x_hbm.at[1], x_ref.at[1]), (first_hbm.at[0], table_ref.at[0]),
        (near_hbm.at[0], near_ref.at[0]), (far_hbm, far_ref),
        (first_hbm.at[rest], table_ref.at[rest]), (near_hbm.at[rest], near_ref.at[rest]),
        (off_hbm, off_ref), (wi_hbm, wi_ref), (lw_hbm, lw_ref), (taps_hbm, taps_ref), (wave_hbm, wave_ref),
    ]
    fetches = [pltpu.make_async_copy(src, dst, in_sem.at[n]) for n, (src, dst) in enumerate(pairs)]
    for fetch in fetches[:5]:
        fetch.start()

    odd = me % 2
    place = (1 - odd) * (me // 2) + odd * (ranks - 1 - me // 2)

    def at_place(p):
        p = (p + ranks) % ranks
        far = p // (ranks // 2)
        return (1 - far) * (2 * p) + far * (2 * (ranks - 1 - p) + 1)

    barrier = pltpu.get_barrier_semaphore()
    for peer in (at_place(place + 1), at_place(place - 1)):
        pl.semaphore_signal(barrier, inc=1, device_id={"freq": peer}, device_id_type=pl.DeviceIdType.MESH)
    pl.semaphore_signal(barrier, inc=1, device_id={"seg": 1 - core}, device_id_type=pl.DeviceIdType.MESH)

    def moved(j, k, way, origin):
        owner = at_place(place - origin) if way == 0 else at_place(place + origin)
        target = at_place(place + 1) if way == 0 else at_place(place - 1)
        classes = pl.ds(0, RADIX) if k < hops - 1 else pl.ds(way * (RADIX // 2), RADIX // 2)
        block = turned_ref.at[j, classes, pl.ds(pl.multiple_of(owner * part, part), part), :]
        return remote(block, block, (ring_send, ring_recv), (way, j, k), "freq", target)

    def send(j, k):
        for way in range(2):
            moved(j, k, way, k).start()

    def landed(j, k):
        for way in range(2):
            moved(j, k, way, k + 1).wait_recv()

    def left(j):
        for k in range(hops):
            for way in range(2):
                moved(j, k, way, k).wait_send()

    own_rows = pl.ds(pl.multiple_of(me * part, part), part)
    for fetch in fetches[:segs]:
        fetch.wait()
    for fetch in fetches[5:]:
        fetch.start()
    for s in range(segs):
        for c in range(comps):
            at = (s * comps + c) * rows
            xb_ref[at : at + rows, :] = x_ref[s, c].astype(BF16)
    for fetch in fetches[2:5]:
        fetch.wait()
    @pl.loop(0, ranks)
    def _(j):
        @pl.when(j == 1)
        def _():
            for fetch in fetches[5:7]:
                fetch.wait()

        first_step(segs, rows, table_ref, xb_ref, near_ref, far_ref, mixed_ref, me, j)
        for n in range(RADIX):
            for i in range(segs * comps):
                lanes = slice(i * BLOCK, (i + 1) * BLOCK)
                turned_ref[j, n, own_rows, lanes] = mixed_ref[i, pl.ds(n, part, stride=RADIX), :].astype(BF16)

        @pl.when(j == 0)
        def _():
            pl.semaphore_wait(barrier, 3)

        @pl.when(j < LEAD)
        def _():
            send(j, 0)

    for fetch in fetches[7:]:
        fetch.wait()
    weights = [lw_ref[wi_ref[s]] * (1.0 / (2 * segs)) for s in range(segs)]
    sift = functools.partial(filter_some, w_ref, band_ref, p_ref, power_ref, off_ref, weights, core * half)

    @pl.loop(0, ranks + hops - 1)
    def _(q):
        @pl.when(q < ranks)
        def _():
            landed(q, 0)
            send(q, 1)

        @pl.when(q < ranks - LEAD)
        def _():
            send(q + LEAD, 0)

        @pl.when(q == 0)
        def _():
            fill_bands(taps_ref, band_ref)

        for k in range(1, hops - 1):

            @pl.when((q >= k) & (q < ranks + k))
            def _():
                landed(q - k, k)
                send(q - k, k + 1)

        for pair in range(ranks // 2 - 1):

            @pl.when(q == 2 * pair + hops + 2)
            def _():
                sift((2 * pair, 2 * pair + 1), rows, ranks, 0, 2 * half)

        @pl.when(q >= hops - 1)
        def _():
            landed(q - hops + 1, hops - 1)
            second_step(segs, wave_ref, turned_ref, w_ref, q - hops + 1)

        @pl.when(q > hops)
        def _():
            left(q - hops - 1)

        @pl.when(q == hops - 1)
        def _():
            wrap_column(w_ref, total)

    def swap(i):
        return remote(send_ref.at[i], got_ref.at[i], (core_send, core_recv), (i,), "seg", 1 - core)

    for part_of in range(2):
        low = half + part_of * (half // 2)
        sift((ranks - 2, ranks - 1), rows, ranks, low, low + half // 2)

        @pl.loop(low - half, low - half + half // 2)
        def _(i):
            t = (1 - core) * half + i
            turns = [source_of(off_ref, s, t, total, ranks)[1] for s in range(segs)]
            for jj in range(ranks):
                x = sum(power_ref[half + i, s, lax.rem(turns[s] + jj, ranks)].astype(F32) for s in range(segs))
                send_ref[i, jj] = x.astype(BF16)
            swap(i).start()

    sift((ranks - 2, ranks - 1), rows, ranks, 0, half)

    for j in range(ranks - 2, ranks):
        left(j)

    for i in range(half):
        swap(i).wait()


def combine_kernel(off_ref, power_ref, got_ref, out_ref, sum_ref, sems):
    half, ranks, rows, _ = got_ref.shape
    segs = power_ref.shape[1]
    core = lax.axis_index("seg")
    copies = []
    for i in range(half):
        turns = [source_of(off_ref, s, core * half + i, rows * ranks, ranks)[1] for s in range(segs)]
        for jj in range(ranks):
            x = got_ref[i, jj].astype(F32)
            for s in range(segs):
                x = x + power_ref[i, s, lax.rem(turns[s] + jj, ranks)].astype(F32)
            sum_ref[i, jj] = x
            copy = pltpu.make_async_copy(sum_ref.at[i, jj], out_ref.at[:, jj, i, :], sems.at[i, jj])
            copy.start()
            copies.append(copy)
    for copy in copies:
        copy.wait()


def body(samples, kernels, offsets, weight_index, level_weights):
    segs, comps, rows, cols = samples.shape
    ranks = lax.axis_size("freq")
    size_one = rows * ranks
    if cols != ranks * BLOCK or rows != BLOCK or size_one != cols or segs != 2 or lax.axis_size("seg") != 2:
        return general(samples, kernels, offsets, weight_index, level_weights)
    length = size_one * cols
    bins = np.arange(cols) - BLOCK // 2
    near = unit(np.arange(rows)[:, None] * bins[None, :] % length / length, 1.0 / math.sqrt(length))
    far = unit(np.arange(ranks)[:, None] * rows * bins[None, :] % length / length)
    count = kernels.shape[1]
    half = count // 2
    tall = rows + PAD
    hops = ranks // 2
    copies = pltpu.SemaphoreType.DMA
    near = np.transpose(np.concatenate(near).reshape(2 * rows, ranks, BLOCK), (1, 0, 2))
    constants = [first_waves(cols), near, np.stack(far, 1), second_waves(size_one)]
    operands = [samples, *(jnp.asarray(x) for x in constants), kernels, offsets, weight_index, level_weights]
    shapes = [pltpu.VMEM(x.shape, x.dtype) for x in operands[:6]] + [pltpu.SMEM(x.shape, x.dtype) for x in operands[6:]]
    power, got = pl.pallas_call(
        gather_kernel,
        out_shape=(
            jax.ShapeDtypeStruct((count, segs, ranks, rows, BLOCK), BF16),
            jax.ShapeDtypeStruct((half, ranks, rows, BLOCK), BF16),
        ),
        in_specs=[pl.BlockSpec(memory_space=pltpu.HBM)] * len(operands),
        out_specs=(VMEM, VMEM),
        scratch_shapes=shapes
        + [
            pltpu.VMEM((segs * comps * rows, cols), BF16),
            pltpu.VMEM((segs * comps, rows, BLOCK), F32),
            pltpu.VMEM((ranks, RADIX, size_one // RADIX, segs * comps * BLOCK), BF16),
            pltpu.VMEM((segs, comps, ranks + 1, size_one + tall, BLOCK), BF16),
            pltpu.VMEM((count, 4 * BLOCK, 2 * BLOCK), BF16),
            pltpu.VMEM((2 * segs * tall, BLOCK), F32),
            pltpu.VMEM((half, ranks, rows, BLOCK), BF16),
        ]
        + [copies((12,))]
        + [copies((2, ranks, hops))] * 2
        + [copies((half,))] * 2,
        compiler_params=pltpu.CompilerParams(vmem_limit_bytes=48 << 20, collective_id=0, has_side_effects=True),
    )(*(pltpu.with_memory_space_constraint(x, pltpu.HBM) for x in operands))
    out = pl.pallas_call(
        combine_kernel,
        out_shape=jax.ShapeDtypeStruct((rows, ranks, half, BLOCK), F32),
        in_specs=[SMEM, VMEM, VMEM],
        out_specs=pl.BlockSpec(memory_space=pltpu.HBM),
        scratch_shapes=[pltpu.VMEM((half, ranks, rows, BLOCK), F32), copies((half, ranks))],
        compiler_params=pltpu.CompilerParams(vmem_limit_bytes=24 << 20),
    )(offsets, power, got)
    return jnp.transpose(out.reshape(rows * ranks, half, BLOCK), (1, 0, 2)).reshape(half, rows * cols)


def solution(mesh):
    in_specs = (
        P(("parts", "seg"), None, "freq", None),
        P(),
        P(("parts", "seg"), None),
        P(("parts", "seg")),
        P(),
    )
    out_specs = P(("parts", "seg"), "freq")
    return jax.shard_map(body, mesh=mesh, in_specs=in_specs, out_specs=out_specs, check_vma=False)
```

```python
import math

import functools

import jax
import jax.numpy as jnp
import numpy as np
from jax import lax
from jax.experimental import pallas as pl
from jax.experimental.pallas import tpu as pltpu
from jax.sharding import PartitionSpec as P

BLOCK = 128
KERNELS = 8
REACH = 4
ROUTE_CAP = 4


def extended(cells, sides, width):
    for axis, dim in sides:
        count = lax.axis_size(axis)
        head = lax.slice_in_dim(cells, 0, width, axis=dim)
        tail = lax.slice_in_dim(cells, cells.shape[dim] - width, cells.shape[dim], axis=dim)
        cells = jnp.concatenate(
            [
                lax.ppermute(tail, axis, [(i, (i + 1) % count) for i in range(count)]),
                cells,
                lax.ppermute(head, axis, [((i + 1) % count, i) for i in range(count)]),
            ],
            axis=dim,
        )
    return cells


def passed_along(block, axis, distance):
    devices = range(lax.axis_size(axis))
    route = [((i - distance) % len(devices), i) for i in devices]
    return lax.ppermute(block, axis, route)


def dft_table(size):
    rows = lax.broadcasted_iota(jnp.int32, (size, size), 0)
    cols = lax.broadcasted_iota(jnp.int32, (size, size), 1)
    angle = (rows * cols % size).astype(jnp.float32) * (2.0 * math.pi / size)
    return (jnp.cos(angle), jnp.sin(angle))


def toeplitz(kernels):
    width = kernels.shape[-1]
    tail = jnp.zeros(kernels.shape[:-1] + (width + 1,), kernels.dtype)
    padded = jnp.concatenate([kernels, tail], -1)
    tiled = jnp.tile(padded, (1, 1, width))[..., : 2 * width * width]
    return tiled.reshape(kernels.shape[:-1] + (width, 2 * width))


def take_blocks(joined, start):
    return lax.dynamic_slice_in_dim(joined, start, joined.shape[0] // 2, 0)


def slide(joined, starts):
    return jax.vmap(jax.vmap(take_blocks))(joined, starts)


def general(samples, kernels, offsets, weight_index, level_weights):
    segs, comps, rows_one, cols_two = samples.shape
    ranks = lax.axis_size("freq")
    here = lax.axis_index("freq")
    size_one = rows_one * ranks
    length = size_one * cols_two
    highest = lax.Precision.HIGHEST
    cos_two, sin_two = dft_table(cols_two)
    stacked = samples.reshape(segs * comps * rows_one, cols_two)
    with_cos = jnp.dot(stacked, cos_two, precision=highest).reshape(samples.shape)
    with_sin = jnp.dot(stacked, sin_two, precision=highest).reshape(samples.shape)
    first_real = with_cos[:, 0] + with_sin[:, 1]
    first_imag = with_cos[:, 1] - with_sin[:, 0]
    row_global = here * rows_one + lax.broadcasted_iota(jnp.int32, (rows_one, cols_two), 0)
    col_global = lax.broadcasted_iota(jnp.int32, (rows_one, cols_two), 1)
    twist = (row_global * col_global % length).astype(jnp.float32) * (2.0 * math.pi / length)
    twist_cos = jnp.cos(twist)
    twist_sin = jnp.sin(twist)
    turned = jnp.stack(
        [
            first_real * twist_cos + first_imag * twist_sin,
            first_imag * twist_cos - first_real * twist_sin,
        ],
        1,
    )
    columns = lax.all_to_all(
        turned.astype(jnp.bfloat16), "freq", split_axis=3, concat_axis=3, tiled=True
    ).astype(turned.dtype)
    width_two = cols_two // ranks
    ordered = columns.reshape(segs, comps, rows_one, ranks, width_two)
    cos_one, sin_one = dft_table(size_one)
    cos_one = cos_one.reshape(ranks, rows_one, size_one)
    sin_one = sin_one.reshape(ranks, rows_one, size_one)
    second_cos = jnp.einsum("scirl,rik->sclk", ordered, cos_one, precision=highest)
    second_sin = jnp.einsum("scirl,rik->sclk", ordered, sin_one, precision=highest)
    second = jnp.stack(
        [second_cos[:, 0] + second_sin[:, 1], second_cos[:, 1] - second_sin[:, 0]], 1
    )
    arrived = lax.all_to_all(
        second.astype(jnp.bfloat16), "freq", split_axis=3, concat_axis=3, tiled=True
    ).astype(second.dtype)
    width_one = size_one // ranks
    spectrum = arrived.reshape(segs, comps, width_two, ranks, width_one)
    spectrum = jnp.transpose(spectrum, (0, 1, 4, 3, 2)).reshape(segs, comps, width_one * cols_two)
    spectrum = (spectrum * (1.0 / math.sqrt(length))).astype(jnp.bfloat16)
    half = BLOCK // 2
    edged = extended(spectrum, (("freq", 2),), half)
    bins_here = spectrum.shape[2]
    count = bins_here // BLOCK
    lower = edged[..., :bins_here].reshape(segs, comps, count, BLOCK)
    upper = edged[..., BLOCK:].reshape(segs, comps, count, BLOCK)
    window = jnp.concatenate([lower, upper], -1)
    bands = toeplitz(kernels)
    real_band = bands[0]
    imag_band = bands[1]
    table = jnp.stack(
        [jnp.stack([real_band, imag_band], 0), jnp.stack([-imag_band, real_band], 0)], 0
    )
    filtered = jnp.einsum("scbm,cokim->skboi", window, table, preferred_element_type=jnp.float32)
    power = (filtered[:, :, :, 0] ** 2 + filtered[:, :, :, 1] ** 2).astype(jnp.bfloat16)
    quotient = jnp.floor_divide(offsets, count)
    remainder = offsets - quotient * count
    following = passed_along(power, "freq", -1)
    inner = slide(jnp.concatenate([power, following], 2), remainder)
    plane_count = segs * KERNELS
    flat = inner.reshape(plane_count, count * BLOCK)
    plane_quot = quotient.reshape(plane_count)
    distances = lax.broadcasted_iota(jnp.int32, (2 * REACH + 1, plane_count), 0) - REACH
    member = (plane_quot[None, :] == distances).astype(jnp.int32)
    earlier = lax.broadcasted_iota(jnp.int32, (plane_count, plane_count), 0)
    later = lax.broadcasted_iota(jnp.int32, (plane_count, plane_count), 1)
    place = jnp.sum(jnp.where(earlier <= later, member[:, :, None], 0), 1) - 1
    slot_ids = lax.broadcasted_iota(jnp.int32, (2 * REACH + 1, ROUTE_CAP, plane_count), 1)
    select = ((member[:, None, :] == 1) & (place[:, None, :] == slot_ids)).astype(jnp.bfloat16)
    packed = jnp.einsum("dcp,pl->dcl", select, flat, preferred_element_type=jnp.float32).astype(
        jnp.bfloat16
    )
    received = []
    for step_index in range(2 * REACH + 1):
        received.append(passed_along(packed[step_index], "freq", -(step_index - REACH)))
    gathered = jnp.stack(received, 0)
    placed = jnp.einsum("dcp,dcl->pl", select, gathered, preferred_element_type=jnp.float32)
    shifted = placed.astype(jnp.bfloat16).reshape(segs, KERNELS, count, BLOCK)
    levels = lax.broadcasted_iota(jnp.int32, (segs, level_weights.shape[0]), 1)
    weights = jnp.sum(jnp.where(weight_index[:, None] == levels, level_weights[None, :], 0.0), 1)
    scale = 1.0 / (segs * lax.axis_size("seg"))
    partial_sum = jnp.sum((weights * scale)[:, None, None, None] * shifted.astype(jnp.float32), 0)
    owned = lax.psum_scatter(
        partial_sum.astype(jnp.bfloat16), "seg", scatter_dimension=0, tiled=True
    ).astype(jnp.float32)
    return owned.reshape(owned.shape[0], count * BLOCK)


VMEM = pl.BlockSpec(memory_space=pltpu.VMEM)
SMEM = pl.BlockSpec(memory_space=pltpu.SMEM)
PAD = 16
RADIX = 4
LEAD = 3
BF16 = jnp.bfloat16
F32 = jnp.float32


def unit(turns, scale=1.0):
    angle = 2.0 * np.pi * turns
    return (np.cos(angle) * scale).astype(np.float32), (np.sin(angle) * scale).astype(np.float32)


def first_waves(size):
    turns = np.arange(size)[:, None] * (np.arange(size) - BLOCK // 2)[None, :] % size / size
    both = np.stack([x.reshape(size, size // BLOCK, BLOCK) for x in unit(turns)], 2)
    return np.transpose(both, (1, 0, 2, 3)).reshape(size // BLOCK, size, 2 * BLOCK).astype(BF16)


def second_waves(size):
    quarter = size // RADIX
    places = np.arange(quarter)[None, None, :] * RADIX + np.arange(RADIX)[:, None, None]
    turns = np.arange(quarter)[None, :, None] * places % size / size
    return np.concatenate(unit(turns), 1).astype(BF16)


def fill_bands(taps_ref, band_ref):
    wide = 2 * BLOCK
    for t in range(taps_ref.shape[1]):
        both = []
        for c in range(2):
            row = taps_ref[c, t : t + 1, :].astype(F32)
            row = jnp.concatenate([row, jnp.zeros_like(row)], 1)
            row = jnp.broadcast_to(row, (BLOCK, wide))
            both.append(pltpu.roll(row, 0, 1, stride=1, stride_axis=0).T)
        re, im = both
        band_ref[t, :wide, :BLOCK] = re.astype(BF16)
        band_ref[t, :wide, BLOCK:] = im.astype(BF16)
        band_ref[t, wide:, :BLOCK] = (-im).astype(BF16)
        band_ref[t, wide:, BLOCK:] = re.astype(BF16)


def remote(src, dst, sems, at, axis, device):
    return pltpu.make_async_remote_copy(
        src_ref=src,
        dst_ref=dst,
        send_sem=sems[0].at[at],
        recv_sem=sems[1].at[at],
        device_id={axis: device},
        device_id_type=pl.DeviceIdType.MESH,
    )


def first_step(segs, rows, table_ref, xb_ref, near_ref, far_ref, mixed_ref, me, j):
    lanes = pl.ds(pl.multiple_of(j * BLOCK, BLOCK), BLOCK)
    got = jnp.dot(xb_ref[...], table_ref[j], preferred_element_type=F32)
    a = far_ref[me, 0:1, lanes]
    b = far_ref[me, 1:2, lanes]
    near_cos = near_ref[j, :rows]
    near_sin = near_ref[j, rows:]
    wc = a * near_cos - b * near_sin
    ws = b * near_cos + a * near_sin
    for s in range(segs):
        top = got[2 * s * rows : (2 * s + 1) * rows]
        low = got[(2 * s + 1) * rows : (2 * s + 2) * rows]
        re = top[:, :BLOCK] + low[:, BLOCK:]
        im = low[:, :BLOCK] - top[:, BLOCK:]
        mixed_ref[2 * s] = re * wc + im * ws
        mixed_ref[2 * s + 1] = im * wc - re * ws


def second_step(segs, wave_ref, turned_ref, w_ref, j):
    wide = 2 * BLOCK
    quarter = wave_ref.shape[1] // 2
    total = quarter * RADIX
    tall = w_ref.shape[3] - total
    for s in range(segs):
        terms = []
        for c in range(RADIX):
            y = jnp.dot(
                wave_ref[c], turned_ref[j, c, :, s * wide : (s + 1) * wide], preferred_element_type=F32
            )
            re = y[:quarter, :BLOCK] + y[quarter:, BLOCK:]
            im = y[:quarter, BLOCK:] - y[quarter:, :BLOCK]
            terms.append((re, im))
        (r0, i0), (r1, i1), (r2, i2), (r3, i3) = terms
        re = (r0 + r2) + (r1 + r3), (r0 - r2) + (i1 - i3), (r0 + r2) - (r1 + r3), (r0 - r2) - (i1 - i3)
        im = (i0 + i2) + (i1 + i3), (i0 - i2) - (r1 - r3), (i0 + i2) - (i1 + i3), (i0 - i2) + (r1 - r3)
        for m in range(RADIX):
            here = slice(m * quarter, (m + 1) * quarter)
            w_ref[s, 0, j, here, :] = re[m].astype(BF16)
            w_ref[s, 1, j, here, :] = im[m].astype(BF16)
        for c in range(2):
            w_ref[s, c, j, total:, :] = w_ref[s, c, j, :tall, :]


def wrap_column(w_ref, total):
    segs, comps, columns, high, _ = w_ref.shape
    for s in range(segs):
        for c in range(comps):
            x = w_ref[s, c, 0, :total, :].astype(F32)
            w_ref[s, c, columns - 1, :total, :] = jnp.concatenate([x[1:], x[:1]], 0).astype(BF16)
            w_ref[s, c, columns - 1, total:, :] = w_ref[s, c, columns - 1, : high - total, :]


def source_of(off_ref, s, t, total, ranks):
    blocks = total * ranks
    base = lax.rem(lax.axis_index("freq") * total + off_ref[s, t] + blocks, blocks)
    return base // ranks, lax.rem(base, ranks)


def filter_some(w_ref, band_ref, p_ref, power_ref, off_ref, weights, first, columns, rows, ranks, low, high):
    segs = len(weights)
    total = rows * ranks
    tall = rows + PAD
    count = band_ref.shape[0]

    @pl.loop(low, high, unroll=min(4, high - low))
    def _(i):
        t = lax.rem(first + i, count)
        parts = []
        shifts = []
        for s in range(segs):
            gk, gj = source_of(off_ref, s, t, total, ranks)
            for j in columns:
                row = lax.rem(gk + (gj - j + ranks - 1) // ranks, total)
                start = row // PAD * PAD
                shifts.append(row - start)
                take = pl.ds(start, tall)
                pieces = [w_ref[s, c, j + e, take, :] for c in range(2) for e in range(2)]
                parts.append(jnp.concatenate(pieces, 1))
        got = jnp.dot(jnp.concatenate(parts, 0), band_ref[t], preferred_element_type=F32)
        re = got[:, :BLOCK]
        im = got[:, BLOCK:]
        p_ref[...] = re * re + im * im
        for s in range(segs):
            for n, j in enumerate(columns):
                at = s * len(columns) + n
                x = p_ref[pl.ds(at * tall + shifts[at], rows), :]
                power_ref[i, s, j] = (weights[s] * x).astype(BF16)


def gather_kernel(
    x_hbm, first_hbm, near_hbm, far_hbm, wave_hbm, taps_hbm, off_hbm, wi_hbm, lw_hbm,
    power_ref, got_ref,
    x_ref, table_ref, near_ref, far_ref, wave_ref, taps_ref, off_ref, wi_ref, lw_ref,
    xb_ref, mixed_ref, turned_ref, w_ref, band_ref, p_ref, send_ref,
    in_sem,
    ring_send, ring_recv, core_send, core_recv,
):
    segs, comps, rows, cols = x_ref.shape
    ranks = lax.axis_size("freq")
    total = rows * ranks
    hops = ranks // 2
    part = rows // RADIX
    me = lax.axis_index("freq")
    core = lax.axis_index("seg")
    half = got_ref.shape[0]

    rest = slice(1, ranks)
    pairs = [
        *((x_hbm.at[s, c], x_ref.at[s, c]) for s in range(segs) for c in range(comps)), (first_hbm.at[0], table_ref.at[0]),
        (near_hbm.at[0], near_ref.at[0]), (far_hbm, far_ref),
        (first_hbm.at[rest], table_ref.at[rest]), (near_hbm.at[rest], near_ref.at[rest]),
        (off_hbm, off_ref), (wi_hbm, wi_ref), (lw_hbm, lw_ref), (taps_hbm, taps_ref), (wave_hbm, wave_ref),
    ]
    fetches = [pltpu.make_async_copy(src, dst, in_sem.at[n]) for n, (src, dst) in enumerate(pairs)]
    for fetch in fetches[:7]:
        fetch.start()

    odd = me % 2
    place = (1 - odd) * (me // 2) + odd * (ranks - 1 - me // 2)

    def at_place(p):
        p = (p + ranks) % ranks
        far = p // (ranks // 2)
        return (1 - far) * (2 * p) + far * (2 * (ranks - 1 - p) + 1)

    barrier = pltpu.get_barrier_semaphore()
    for peer in (at_place(place + 1), at_place(place - 1)):
        pl.semaphore_signal(barrier, inc=1, device_id={"freq": peer}, device_id_type=pl.DeviceIdType.MESH)
    pl.semaphore_signal(barrier, inc=1, device_id={"seg": 1 - core}, device_id_type=pl.DeviceIdType.MESH)

    def moved(j, k, way, origin):
        owner = at_place(place - origin) if way == 0 else at_place(place + origin)
        target = at_place(place + 1) if way == 0 else at_place(place - 1)
        classes = pl.ds(0, RADIX) if k < hops - 1 else pl.ds(way * (RADIX // 2), RADIX // 2)
        block = turned_ref.at[j, classes, pl.ds(pl.multiple_of(owner * part, part), part), :]
        return remote(block, block, (ring_send, ring_recv), (way, j, k), "freq", target)

    def send(j, k):
        for way in range(2):
            moved(j, k, way, k).start()

    def landed(j, k):
        for way in range(2):
            moved(j, k, way, k + 1).wait_recv()

    def left(j):
        for k in range(hops):
            for way in range(2):
                moved(j, k, way, k).wait_send()

    own_rows = pl.ds(pl.multiple_of(me * part, part), part)
    for s in range(segs):
        for c in range(comps):
            fetches[s * comps + c].wait()
            at = (s * comps + c) * rows
            xb_ref[at : at + rows, :] = x_ref[s, c].astype(BF16)
    for fetch in fetches[4:7]:
        fetch.wait()
    for fetch in fetches[7:]:
        fetch.start()
    @pl.loop(0, ranks)
    def _(j):
        @pl.when(j == 1)
        def _():
            for fetch in fetches[7:9]:
                fetch.wait()

        first_step(segs, rows, table_ref, xb_ref, near_ref, far_ref, mixed_ref, me, j)
        for n in range(RADIX):
            for i in range(segs * comps):
                lanes = slice(i * BLOCK, (i + 1) * BLOCK)
                turned_ref[j, n, own_rows, lanes] = mixed_ref[i, pl.ds(n, part, stride=RADIX), :].astype(BF16)

        @pl.when(j == 0)
        def _():
            pl.semaphore_wait(barrier, 3)

        @pl.when(j < LEAD)
        def _():
            send(j, 0)

    for fetch in fetches[9:]:
        fetch.wait()
    weights = [lw_ref[wi_ref[s]] * (1.0 / (2 * segs)) for s in range(segs)]
    sift = functools.partial(filter_some, w_ref, band_ref, p_ref, power_ref, off_ref, weights, core * half)

    @pl.loop(0, ranks + hops - 1)
    def _(q):
        @pl.when(q < ranks)
        def _():
            landed(q, 0)
            send(q, 1)

        @pl.when(q < ranks - LEAD)
        def _():
            send(q + LEAD, 0)

        @pl.when(q == 0)
        def _():
            fill_bands(taps_ref, band_ref)

        for k in range(1, hops - 1):

            @pl.when((q >= k) & (q < ranks + k))
            def _():
                landed(q - k, k)
                send(q - k, k + 1)

        for pair in range(ranks // 2 - 1):

            @pl.when(q == 2 * pair + hops + 2)
            def _():
                sift((2 * pair, 2 * pair + 1), rows, ranks, 0, 2 * half)

        @pl.when(q >= hops - 1)
        def _():
            landed(q - hops + 1, hops - 1)
            second_step(segs, wave_ref, turned_ref, w_ref, q - hops + 1)

        @pl.when(q > hops)
        def _():
            left(q - hops - 1)

        @pl.when(q == hops - 1)
        def _():
            wrap_column(w_ref, total)

    def swap(i):
        return remote(send_ref.at[i], got_ref.at[i], (core_send, core_recv), (i,), "seg", 1 - core)

    for part_of in range(2):
        low = half + part_of * (half // 2)
        sift((ranks - 2, ranks - 1), rows, ranks, low, low + half // 2)

        for i in range(low - half, low - half + half // 2):
            t = (1 - core) * half + i
            turns = [source_of(off_ref, s, t, total, ranks)[1] for s in range(segs)]
            for jj in range(ranks):
                x = sum(power_ref[half + i, s, lax.rem(turns[s] + jj, ranks)].astype(F32) for s in range(segs))
                send_ref[i, jj] = x.astype(BF16)
            swap(i).start()

    sift((ranks - 2, ranks - 1), rows, ranks, 0, half)

    for j in range(ranks - 2, ranks):
        left(j)

    for i in range(half):
        swap(i).wait()


def combine_kernel(off_ref, power_ref, got_ref, out_ref, sum_ref, sems):
    half, ranks, rows, _ = got_ref.shape
    segs = power_ref.shape[1]
    core = lax.axis_index("seg")
    copies = []
    for i in range(half):
        turns = [source_of(off_ref, s, core * half + i, rows * ranks, ranks)[1] for s in range(segs)]
        for jj in range(ranks):
            x = got_ref[i, jj].astype(F32)
            for s in range(segs):
                x = x + power_ref[i, s, lax.rem(turns[s] + jj, ranks)].astype(F32)
            sum_ref[i, jj] = x
            copy = pltpu.make_async_copy(sum_ref.at[i, jj], out_ref.at[:, jj, i, :], sems.at[i, jj])
            copy.start()
            copies.append(copy)
    for copy in copies:
        copy.wait()


def body(samples, kernels, offsets, weight_index, level_weights):
    segs, comps, rows, cols = samples.shape
    ranks = lax.axis_size("freq")
    size_one = rows * ranks
    if cols != ranks * BLOCK or rows != BLOCK or size_one != cols or segs != 2 or lax.axis_size("seg") != 2:
        return general(samples, kernels, offsets, weight_index, level_weights)
    length = size_one * cols
    bins = np.arange(cols) - BLOCK // 2
    near = unit(np.arange(rows)[:, None] * bins[None, :] % length / length, 1.0 / math.sqrt(length))
    far = unit(np.arange(ranks)[:, None] * rows * bins[None, :] % length / length)
    count = kernels.shape[1]
    half = count // 2
    tall = rows + PAD
    hops = ranks // 2
    copies = pltpu.SemaphoreType.DMA
    near = np.transpose(np.concatenate(near).reshape(2 * rows, ranks, BLOCK), (1, 0, 2))
    constants = [first_waves(cols), near, np.stack(far, 1), second_waves(size_one)]
    operands = [samples, *(jnp.asarray(x) for x in constants), kernels, offsets, weight_index, level_weights]
    shapes = [pltpu.VMEM(x.shape, x.dtype) for x in operands[:6]] + [pltpu.SMEM(x.shape, x.dtype) for x in operands[6:]]
    power, got = pl.pallas_call(
        gather_kernel,
        out_shape=(
            jax.ShapeDtypeStruct((count, segs, ranks, rows, BLOCK), BF16),
            jax.ShapeDtypeStruct((half, ranks, rows, BLOCK), BF16),
        ),
        in_specs=[pl.BlockSpec(memory_space=pltpu.HBM)] * len(operands),
        out_specs=(VMEM, VMEM),
        scratch_shapes=shapes
        + [
            pltpu.VMEM((segs * comps * rows, cols), BF16),
            pltpu.VMEM((segs * comps, rows, BLOCK), F32),
            pltpu.VMEM((ranks, RADIX, size_one // RADIX, segs * comps * BLOCK), BF16),
            pltpu.VMEM((segs, comps, ranks + 1, size_one + tall, BLOCK), BF16),
            pltpu.VMEM((count, 4 * BLOCK, 2 * BLOCK), BF16),
            pltpu.VMEM((2 * segs * tall, BLOCK), F32),
            pltpu.VMEM((half, ranks, rows, BLOCK), BF16),
        ]
        + [copies((14,))]
        + [copies((2, ranks, hops))] * 2
        + [copies((half,))] * 2,
        compiler_params=pltpu.CompilerParams(vmem_limit_bytes=48 << 20, collective_id=0, has_side_effects=True),
    )(*(pltpu.with_memory_space_constraint(x, pltpu.HBM) for x in operands))
    out = pl.pallas_call(
        combine_kernel,
        out_shape=jax.ShapeDtypeStruct((rows, ranks, half, BLOCK), F32),
        in_specs=[SMEM, VMEM, VMEM],
        out_specs=pl.BlockSpec(memory_space=pltpu.HBM),
        scratch_shapes=[pltpu.VMEM((half, ranks, rows, BLOCK), F32), copies((half, ranks))],
        compiler_params=pltpu.CompilerParams(vmem_limit_bytes=24 << 20),
    )(offsets, power, got)
    return jnp.transpose(out.reshape(rows * ranks, half, BLOCK), (1, 0, 2)).reshape(half, rows * cols)


def solution(mesh):
    in_specs = (
        P(("parts", "seg"), None, "freq", None),
        P(),
        P(("parts", "seg"), None),
        P(("parts", "seg")),
        P(),
    )
    out_specs = P(("parts", "seg"), "freq")
    return jax.shard_map(body, mesh=mesh, in_specs=in_specs, out_specs=out_specs, check_vma=False)
```
